256 devices in a mesh: date: 64 (over z, x, core), pix: 4 (over y).
Axes of the slice: x: 4, y: 4, z: 8, core: 2. Of those that a mesh axis runs over, the one named last changes fastest.
Arguments:
- stack: bfloat16 [64, 10, 32, 2048], P('date', None, 'pix'), may hold values from -4 to 12
- cloud: int32 [64, 32, 2048], P('date', 'pix'), may hold values 0 or 1
Outputs:
- composite: float32 [10, 32, 2048], P(None, 'pix')
The draws below stay inside these ranges and needn't reach their ends.
All inputs are finite; a program needn't handle non-finite values. No bound on the sum of `cloud` on one device may be relied on, other than what follows from the above.
Results may differ from the reference program's by a relative error of at most 0.0003.
Values may be sent and summed in bfloat16 or wider, within the bound.
A program may use at most 64 MiB of HBM per device.

```python
import jax
import jax.numpy as jnp
from jax import lax

BANDS = 10
ROWS_DEV = 8
COLS = 2048
ITERS = 2
DATES = 64
NROWS = 32


def draw_stack(key, part):
    keys = jax.random.split(jax.random.fold_in(key, 17), 5)
    rows = jnp.arange(NROWS, dtype=jnp.float32)
    bright = 1.0 + 2.0 * rows / max(NROWS - 1, 1)
    band_base = jax.random.uniform(keys[0], (BANDS,), jnp.float32, 0.5, 1.5)
    surface = jax.random.normal(keys[1], (BANDS, NROWS, COLS), jnp.float32)
    noise = jax.random.normal(keys[2], (DATES, BANDS, NROWS, COLS), jnp.float32)
    hazy = jax.random.bernoulli(keys[3], 0.1, (DATES, 1, NROWS, COLS)).astype(jnp.float32)
    haze = hazy * jax.random.uniform(keys[4], (DATES, 1, NROWS, COLS), jnp.float32, 1.0, 3.0)
    ground = bright[None, :, None] * band_base[:, None, None] * (1.0 + 0.3 * surface)
    values = ground[None] + noise + haze
    return jnp.clip(values, -4.0, 12.0).astype(jnp.bfloat16)


def place_ends(drawn, key, least, high):
    spot = [jax.random.randint(jax.random.fold_in(key, axis), (), 0, length) for axis, length in enumerate(drawn.shape)]
    longest = drawn.shape.index(max(drawn.shape))
    next_to = spot[:longest] + [(spot[longest] + 1) % drawn.shape[longest]] + spot[longest + 1:]
    return drawn.at[tuple(spot)].set(least).at[tuple(next_to)].set(high)


def setup_inputs(seed: int = 0) -> dict:
    seeds = jax.random.split(jax.random.key(seed), 3)
    return {
        "stack": draw_stack(jax.random.fold_in(seeds[2], 71), 0),
        "cloud": place_ends((jax.random.randint(seeds[1], (DATES, NROWS, COLS), 0, 4) < 3).astype(jnp.int32), jax.random.fold_in(seeds[1], 1), 0, 1),
    }


delta_sq = 0.01
eps = 1e-05

def clear_flags(cloud):
    cloudy = (1 - cloud).astype(jnp.float32)
    padded = jnp.pad(cloudy, ((0, 0), (1, 1), (1, 1)))
    near = jnp.maximum(padded[:, 1:-1, 1:-1], padded[:, 2:, 1:-1])
    near = jnp.maximum(near, padded[:, :-2, 1:-1])
    near = jnp.maximum(near, padded[:, 1:-1, 2:])
    near = jnp.maximum(near, padded[:, 1:-1, :-2])
    return 1.0 - near

def median_block(block, valid):
    values = block.astype(jnp.float32)
    median = jnp.zeros(values.shape[1:], jnp.float32)
    for step in range(ITERS + 1):
        if step == 0:
            weight = valid
        else:
            diff = values - median[None]
            weight = valid / jnp.sqrt(lax.optimization_barrier(jnp.sum(diff * diff, axis=1)) + delta_sq)
        numer = lax.optimization_barrier(jnp.sum(weight[:, None] * values, axis=0))
        denom = lax.optimization_barrier(jnp.sum(weight, axis=0))
        median = (numer + median) / (denom + 1.0)
    return median

def reference(stack, cloud):
    valid = clear_flags(cloud)
    blocks = NROWS // ROWS_DEV

    def one_block(index):
        start = (index * ROWS_DEV).astype(jnp.int32)
        part = lax.dynamic_slice_in_dim(stack, start, ROWS_DEV, 2)
        flags = lax.dynamic_slice_in_dim(valid, start, ROWS_DEV, 1)
        return median_block(part, flags)
    pieces = lax.map(one_block, jnp.arange(blocks, dtype=jnp.int32))
    median = jnp.transpose(pieces, (1, 0, 2, 3)).reshape(BANDS, NROWS, COLS)
    count = NROWS * COLS
    mean = lax.optimization_barrier(jnp.sum(median, axis=(1, 2))) / count
    var = lax.optimization_barrier(jnp.sum(median * median, axis=(1, 2))) / count - mean * mean
    return (median - mean[:, None, None]) / jnp.sqrt(var[:, None, None] + eps)
```

```python
import functools

import jax
import jax.numpy as jnp
from jax import lax
from jax.experimental import pallas as pl
from jax.experimental.pallas import tpu as pltpu
from jax.sharding import PartitionSpec as P

ITERS = 2
DELTA_SQ = 0.01
EPS = 1e-05
MESH = pl.DeviceIdType.MESH
Z, X, CORE, Y = 8, 4, 2, 4
PEERS = Z * X * CORE
PAIRS = 4
LANES = 128


def kernel(
    pixels, stack_ref, cloud_ref, out_ref,
    send, recv, hsend, hrecv, vsend, vrecv, work, seen, gath, part, ymom, dmom,
    s_stack, r_stack, s_halo, r_halo, s_valid, r_valid,
    s_z, s_x, s_core, r_gath, s_ymom, r_ymom, s_dmom, r_dmom,
):
    bands = stack_ref.shape[0]
    rows, cols = cloud_ref.shape
    me = lax.axis_index("date")
    y = lax.axis_index("pix")
    z = me // (X * CORE)
    x = (me // CORE) % X
    core = me % CORE

    def date_at(zz, xx, cc):
        return (zz * X + xx) * CORE + cc

    def peer(step):
        return (me + step) % PEERS

    barrier = pltpu.get_barrier_semaphore()

    @pl.loop(1, PEERS)
    def _(step):
        pl.semaphore_signal(barrier, inc=1, device_id={"date": peer(step)}, device_id_type=MESH)

    for step in range(1, Y):
        pl.semaphore_signal(barrier, inc=1, device_id={"pix": (y + step) % Y}, device_id_type=MESH)

    @pl.loop(0, Z)
    def _(zz):
        for cc in range(CORE):
            tile = pl.ds(pl.multiple_of((zz * CORE + cc) * LANES, LANES), LANES)
            for k in range(PAIRS):
                send[date_at(zz, k, cc)] = stack_ref[:, 2 * k : 2 * k + 2, tile]

    recv[me] = send[me]
    cloudy = (1 - cloud_ref[...]).astype(jnp.float32)
    hsend[0] = cloudy[0:1]
    hsend[1] = cloudy[rows - 1 : rows]

    pl.semaphore_wait(barrier, PEERS - 1 + Y - 1)

    halos = []
    for side, to in ((0, (y + Y - 1) % Y), (1, (y + 1) % Y)):
        halos.append(
            pltpu.make_async_remote_copy(
                src_ref=hsend.at[side], dst_ref=hrecv.at[side],
                send_sem=s_halo.at[side], recv_sem=r_halo.at[side],
                device_id={"pix": to}, device_id_type=MESH,
            )
        )
    for copy in halos:
        copy.start()

    @pl.loop(1, PEERS)
    def _(step):
        to = peer(step)
        pltpu.make_async_remote_copy(
            src_ref=send.at[to], dst_ref=recv.at[me], send_sem=s_stack, recv_sem=r_stack.at[me],
            device_id={"date": to}, device_id_type=MESH,
        ).start()

    for copy in halos:
        copy.wait()
    above = jnp.where(y > 0, hrecv[1], 0.0)
    below = jnp.where(y < Y - 1, hrecv[0], 0.0)
    row = lax.broadcasted_iota(jnp.int32, (rows, cols), 0)
    col = lax.broadcasted_iota(jnp.int32, (rows, cols), 1)
    near = jnp.maximum(cloudy, jnp.where(row == 0, above, pltpu.roll(cloudy, 1, 0)))
    near = jnp.maximum(near, jnp.where(row == rows - 1, below, pltpu.roll(cloudy, rows - 1, 0)))
    near = jnp.maximum(near, jnp.where(col == 0, 0.0, pltpu.roll(cloudy, 1, 1)))
    near = jnp.maximum(near, jnp.where(col == cols - 1, 0.0, pltpu.roll(cloudy, cols - 1, 1)))
    valid = 1.0 - near
    for c in range(Z * CORE):
        for k in range(PAIRS):
            block = valid[2 * k : 2 * k + 2, c * LANES : (c + 1) * LANES]
            vsend[date_at(c // CORE, k, c % CORE)] = block.astype(jnp.bfloat16)
    vrecv[me] = vsend[me]

    @pl.loop(1, PEERS)
    def _(step):
        to = peer(step)
        pltpu.make_async_remote_copy(
            src_ref=vsend.at[to], dst_ref=vrecv.at[me], send_sem=s_valid, recv_sem=r_valid.at[me],
            device_id={"date": to}, device_id_type=MESH,
        ).start()

    @pl.loop(0, PEERS)
    def _(step):
        date = peer(step)

        @pl.when(step > 0)
        def _():
            pltpu.make_async_copy(recv.at[date], recv.at[date], r_stack.at[date]).wait()

        block = recv[date].astype(jnp.float32)
        for b in range(bands):
            for r in range(2):
                work[r, b, pl.ds(date, 1), :] = block[b, r : r + 1]

    @pl.loop(0, PEERS)
    def _(step):
        date = peer(step)

        @pl.when(step > 0)
        def _():
            pltpu.make_async_copy(vrecv.at[date], vrecv.at[date], r_valid.at[date]).wait()

        block = vrecv[date].astype(jnp.float32)
        for r in range(2):
            seen[r, pl.ds(date, 1), :] = block[r : r + 1]

    @pl.loop(0, 2)
    def _(r):
        median = [jnp.zeros((1, LANES), jnp.float32)] * bands
        for step in range(ITERS + 1):
            numer = [jnp.zeros((8, LANES), jnp.float32)] * bands
            denom = jnp.zeros((8, LANES), jnp.float32)
            for j in range(0, PEERS, 8):
                values = [work[r, b, j : j + 8, :] for b in range(bands)]
                weight = seen[r, j : j + 8, :]
                if step > 0:
                    square = DELTA_SQ
                    for b in range(bands):
                        diff = values[b] - median[b]
                        square = square + diff * diff
                    weight = weight * lax.rsqrt(square)
                denom = denom + weight
                numer = [n + weight * v for n, v in zip(numer, values)]
            scale = 1.0 / (jnp.sum(denom, axis=0, keepdims=True) + 1.0)
            median = [
                (jnp.sum(n, axis=0, keepdims=True) + m) * scale for n, m in zip(numer, median)
            ]
        for b in range(bands):
            gath[core, x, z, b, pl.ds(r, 1), :] = median[b]
            part[r, b : b + 1, :] = median[b]
            part[r, bands + b : bands + b + 1, :] = median[b] * median[b]

    def pass_on(chunk, send_sem, to):
        pltpu.make_async_remote_copy(
            src_ref=gath.at[chunk], dst_ref=gath.at[chunk],
            send_sem=send_sem, recv_sem=r_gath.at[chunk],
            device_id={"date": to}, device_id_type=MESH,
        ).start()

    def arrived(chunk):
        pltpu.make_async_copy(gath.at[chunk], gath.at[chunk], r_gath.at[chunk]).wait()

    for step in (1, 7, 2, 6, 3, 5, 4):
        pass_on((core, x, z), s_z, date_at((z + step) % Z, x, core))
    for step in (1, 3, 2):
        pass_on((core, x, z), s_x, date_at(z, (x + step) % X, core))
    pass_on((core, x, z), s_core, date_at(z, x, 1 - core))

    sums = jnp.sum(part[0] + part[1], axis=1, keepdims=True)
    lane = lax.broadcasted_iota(jnp.int32, (2 * bands, LANES), 1)
    which = lax.broadcasted_iota(jnp.int32, (2 * bands, LANES), 0)
    ymom[y] = jnp.sum(jnp.where(lane == which, sums, 0.0), axis=0, keepdims=True)
    for step in range(1, Y):
        pltpu.make_async_remote_copy(
            src_ref=ymom.at[y], dst_ref=ymom.at[y], send_sem=s_ymom, recv_sem=r_ymom.at[y],
            device_id={"pix": (y + step) % Y}, device_id_type=MESH,
        ).start()
    for step in range(1, Y):
        other = (y + step) % Y
        pltpu.make_async_copy(ymom.at[other], ymom.at[other], r_ymom.at[other]).wait()
    dmom[me] = (ymom[0] + ymom[1]) + (ymom[2] + ymom[3])

    @pl.loop(1, PEERS)
    def _(step):
        to = peer(step)
        pltpu.make_async_remote_copy(
            src_ref=dmom.at[me], dst_ref=dmom.at[me], send_sem=s_dmom, recv_sem=r_dmom.at[me],
            device_id={"date": to}, device_id_type=MESH,
        ).start()

    for step in (1, 7, 2, 6, 3, 5, 4):
        chunk = (core, x, (z + step) % Z)
        arrived(chunk)
        for hop in (1, 3, 2):
            pass_on(chunk, s_x, date_at(z, (x + hop) % X, core))
        pass_on(chunk, s_core, date_at(z, x, 1 - core))
    for step in (0, 1, 7, 2, 6, 3, 5, 4):
        for hop in (1, 3, 2):
            chunk = (core, (x + hop) % X, (z + step) % Z)
            arrived(chunk)
            pass_on(chunk, s_core, date_at(z, x, 1 - core))

    @pl.loop(1, PEERS)
    def _(step):
        date = peer(step)
        pltpu.make_async_copy(dmom.at[date], dmom.at[date], r_dmom.at[date]).wait()

    total = dmom[0]
    for d in range(1, PEERS):
        total = total + dmom[d]
    lane = lax.broadcasted_iota(jnp.int32, (1, LANES), 1)
    means, scales = [], []
    for b in range(bands):
        mean = jnp.sum(jnp.where(lane == b, total, 0.0), axis=1, keepdims=True) / pixels
        second = jnp.sum(jnp.where(lane == bands + b, total, 0.0), axis=1, keepdims=True) / pixels
        var = second - mean * mean
        means.append(mean)
        scales.append(1.0 / jnp.sqrt(var + EPS))

    @pl.loop(0, X)
    def _(xx):
        @pl.loop(0, Z)
        def _(zz):
            arrived((1 - core, xx, zz))

    @pl.loop(0, Z)
    def _(zz):
        for cc in range(CORE):
            tile = pl.ds(pl.multiple_of((zz * CORE + cc) * LANES, LANES), LANES)
            for b in range(bands):
                block = jnp.concatenate([gath[cc, k, zz, b] for k in range(PAIRS)], axis=0)
                out_ref[b, :, tile] = (block - means[b]) * scales[b]

    pltpu.make_async_copy(send.at[pl.ds(0, PEERS - 1)], send.at[pl.ds(0, PEERS - 1)], s_stack).wait()
    pltpu.make_async_copy(vsend.at[pl.ds(0, PEERS - 1)], vsend.at[pl.ds(0, PEERS - 1)], s_valid).wait()
    pltpu.make_async_copy(dmom.at[pl.ds(0, PEERS - 1)], dmom.at[pl.ds(0, PEERS - 1)], s_dmom).wait()
    pltpu.make_async_copy(ymom.at[pl.ds(0, Y - 1)], ymom.at[pl.ds(0, Y - 1)], s_ymom).wait()
    z_sent = gath.at[0, 0, pl.ds(0, Z - 1)]
    pltpu.make_async_copy(z_sent, z_sent, s_z).wait()
    x_sent = gath.at[0, pl.ds(0, X - 1)]
    pltpu.make_async_copy(x_sent, x_sent, s_x).wait()
    pltpu.make_async_copy(gath.at[0], gath.at[0], s_core).wait()


def body(stack, cloud):
    _, bands, rows, cols = stack.shape
    pixels = float(lax.axis_size("pix") * rows * cols)
    f32, bf16 = jnp.float32, jnp.bfloat16
    dma = pltpu.SemaphoreType.DMA
    return pl.pallas_call(
        functools.partial(kernel, pixels),
        out_shape=jax.ShapeDtypeStruct((bands, rows, cols), f32),
        in_specs=[pl.BlockSpec(memory_space=pltpu.VMEM)] * 2,
        out_specs=pl.BlockSpec(memory_space=pltpu.VMEM),
        scratch_shapes=[
            pltpu.VMEM((PEERS, bands, 2, LANES), bf16),
            pltpu.VMEM((PEERS, bands, 2, LANES), bf16),
            pltpu.VMEM((2, 1, cols), f32),
            pltpu.VMEM((2, 1, cols), f32),
            pltpu.VMEM((PEERS, 2, LANES), bf16),
            pltpu.VMEM((PEERS, 2, LANES), bf16),
            pltpu.VMEM((2, bands, PEERS, LANES), f32),
            pltpu.VMEM((2, PEERS, LANES), f32),
            pltpu.VMEM((CORE, X, Z, bands, 2, LANES), f32),
            pltpu.VMEM((2, 2 * bands, LANES), f32),
            pltpu.VMEM((Y, 1, LANES), f32),
            pltpu.VMEM((PEERS, 1, LANES), f32),
            dma, dma((PEERS,)), dma((2,)), dma((2,)), dma, dma((PEERS,)),
            dma, dma, dma, dma((CORE, X, Z)), dma, dma((Y,)), dma, dma((PEERS,)),
        ],
        compiler_params=pltpu.CompilerParams(collective_id=0, has_side_effects=True),
    )(stack[0], cloud[0])


def solution(mesh):
    placed = (P("date", None, "pix", None), P("date", "pix", None))
    return jax.shard_map(
        body, mesh=mesh, in_specs=placed, out_specs=P(None, "pix", None), check_vma=False
    )
```

```python
import functools

import jax
import jax.numpy as jnp
from jax import lax
from jax.experimental import pallas as pl
from jax.experimental.pallas import tpu as pltpu
from jax.sharding import PartitionSpec as P

ITERS = 2
DELTA_SQ = 0.01
EPS = 1e-05
MESH = pl.DeviceIdType.MESH
Z, X, CORE, Y = 8, 4, 2, 4
LINE = X * CORE
PEERS = Z * LINE
PAIRS = 4
LANES = 128


def kernel(
    pixels, stack_hbm, cloud_hbm, out_ref,
    stack_ref, cloud_ref, send, recv, hsend, hrecv, vsend, vrecv, work, seen, gath, part, ymom, dmom,
    s_stack, r_stack, s_halo, r_halo, s_valid, r_valid,
    s_z, s_x, s_core, r_z, r_x, r_core, s_ymom, r_ymom, s_dmom, r_dmom,
    s_in,
):
    bands = stack_ref.shape[0]
    rows, cols = cloud_ref.shape
    me = lax.axis_index("date")
    y = lax.axis_index("pix")
    z = me // (X * CORE)
    x = (me // CORE) % X
    core = me % CORE

    def date_at(zz, xx, cc):
        return (zz * X + xx) * CORE + cc

    def peer(step):
        return (me + step) % PEERS

    def in_line(zz, step):
        return zz * LINE + (me % LINE + step) % LINE

    def give(zz, first):
        @pl.loop(first, LINE)
        def _(step):
            to = in_line(zz, step)
            pltpu.make_async_remote_copy(
                src_ref=send.at[to], dst_ref=recv.at[me],
                send_sem=s_stack, recv_sem=r_stack.at[z],
                device_id={"date": to}, device_id_type=MESH,
            ).start()

    fetches = [
        pltpu.make_async_copy(cloud_hbm, cloud_ref, s_in.at[0]),
        pltpu.make_async_copy(stack_hbm, stack_ref, s_in.at[1]),
    ]

    barrier = pltpu.get_barrier_semaphore()
    for copy in fetches:
        copy.start()

    @pl.loop(1, PEERS)
    def _(step):
        pl.semaphore_signal(barrier, inc=1, device_id={"date": peer(step)}, device_id_type=MESH)

    for step in range(1, Y):
        pl.semaphore_signal(barrier, inc=1, device_id={"pix": (y + step) % Y}, device_id_type=MESH)

    for copy in fetches:
        copy.wait()

    @pl.loop(0, Z)
    def _(zz):
        for cc in range(CORE):
            tile = pl.ds(pl.multiple_of((zz * CORE + cc) * LANES, LANES), LANES)
            for k in range(PAIRS):
                send[date_at(zz, k, cc)] = stack_ref[:, 2 * k : 2 * k + 2, tile]

    recv[me] = send[me]
    cloudy = (1 - cloud_ref[...]).astype(jnp.float32)
    hsend[0] = cloudy[0:1]
    hsend[1] = cloudy[rows - 1 : rows]

    pl.semaphore_wait(barrier, PEERS - 1 + Y - 1)

    halos = []
    for side, to in ((0, (y + Y - 1) % Y), (1, (y + 1) % Y)):
        halos.append(
            pltpu.make_async_remote_copy(
                src_ref=hsend.at[side], dst_ref=hrecv.at[side],
                send_sem=s_halo.at[side], recv_sem=r_halo.at[side],
                device_id={"pix": to}, device_id_type=MESH,
            )
        )
    for copy in halos:
        copy.start()

    for dz in (4, 3, 5, 2, 6, 1, 7):
        give((z + dz) % Z, 0)
    give(z, 1)

    for copy in halos:
        copy.wait()
    above = jnp.where(y > 0, hrecv[1], 0.0)
    below = jnp.where(y < Y - 1, hrecv[0], 0.0)
    row = lax.broadcasted_iota(jnp.int32, (rows, cols), 0)
    col = lax.broadcasted_iota(jnp.int32, (rows, cols), 1)
    near = jnp.maximum(cloudy, jnp.where(row == 0, above, pltpu.roll(cloudy, 1, 0)))
    near = jnp.maximum(near, jnp.where(row == rows - 1, below, pltpu.roll(cloudy, rows - 1, 0)))
    near = jnp.maximum(near, jnp.where(col == 0, 0.0, pltpu.roll(cloudy, 1, 1)))
    near = jnp.maximum(near, jnp.where(col == cols - 1, 0.0, pltpu.roll(cloudy, cols - 1, 1)))
    valid = 1.0 - near
    for c in range(Z * CORE):
        for k in range(PAIRS):
            block = valid[2 * k : 2 * k + 2, c * LANES : (c + 1) * LANES]
            vsend[date_at(c // CORE, k, c % CORE)] = block.astype(jnp.bfloat16)
    vrecv[me] = vsend[me]

    @pl.loop(1, PEERS)
    def _(step):
        to = peer(step)
        pltpu.make_async_remote_copy(
            src_ref=vsend.at[to], dst_ref=vrecv.at[me], send_sem=s_valid, recv_sem=r_valid,
            device_id={"date": to}, device_id_type=MESH,
        ).start()

    def taken(ref, count, sem):
        some = ref.at[pl.ds(0, count)]
        pltpu.make_async_copy(some, some, sem).wait()

    def unpack(zz):
        @pl.loop(0, LINE)
        def _(step):
            date = zz * LINE + step
            block = recv[date].astype(jnp.float32)
            for b in range(bands):
                for r in range(2):
                    work[r, b, pl.ds(date, 1), :] = block[b, r : r + 1]

    taken(recv, LINE - 1, r_stack.at[z])
    unpack(z)

    @pl.loop(1, Z)
    def _(step):
        zz = (z + step) % Z
        taken(recv, LINE, r_stack.at[zz])
        unpack(zz)

    taken(vrecv, PEERS - 1, r_valid)

    @pl.loop(0, PEERS)
    def _(date):
        block = vrecv[date].astype(jnp.float32)
        for r in range(2):
            seen[r, pl.ds(date, 1), :] = block[r : r + 1]

    @pl.loop(0, 2)
    def _(r):
        median = [jnp.zeros((1, LANES), jnp.float32)] * bands
        for step in range(ITERS + 1):
            numer = [jnp.zeros((8, LANES), jnp.float32)] * bands
            denom = jnp.zeros((8, LANES), jnp.float32)
            for j in range(0, PEERS, 8):
                values = [work[r, b, j : j + 8, :] for b in range(bands)]
                weight = seen[r, j : j + 8, :]
                if step > 0:
                    square = DELTA_SQ
                    for b in range(bands):
                        diff = values[b] - median[b]
                        square = square + diff * diff
                    weight = weight * lax.rsqrt(square)
                denom = denom + weight
                numer = [n + weight * v for n, v in zip(numer, values)]
            scale = 1.0 / (jnp.sum(denom, axis=0, keepdims=True) + 1.0)
            median = [
                (jnp.sum(n, axis=0, keepdims=True) + m) * scale for n, m in zip(numer, median)
            ]
        for b in range(bands):
            gath[core, x, z, b, pl.ds(r, 1), :] = median[b]
            part[r, b : b + 1, :] = median[b]
            part[r, bands + b : bands + b + 1, :] = median[b] * median[b]

    def pass_on(chunk, send_sem, recv_sem, to):
        pltpu.make_async_remote_copy(
            src_ref=gath.at[chunk], dst_ref=gath.at[chunk],
            send_sem=send_sem, recv_sem=recv_sem,
            device_id={"date": to}, device_id_type=MESH,
        ).start()

    for step in (1, 7, 2, 6, 3, 5, 4):
        pass_on((core, x, z), s_z, r_z.at[z], date_at((z + step) % Z, x, core))
    for step in (1, 3, 2):
        pass_on((core, x, z), s_x, r_x.at[z], date_at(z, (x + step) % X, core))
    pass_on((core, x, z), s_core, r_core, date_at(z, x, 1 - core))

    sums = jnp.sum(part[0] + part[1], axis=1, keepdims=True)
    lane = lax.broadcasted_iota(jnp.int32, (2 * bands, LANES), 1)
    which = lax.broadcasted_iota(jnp.int32, (2 * bands, LANES), 0)
    ymom[y] = jnp.sum(jnp.where(lane == which, sums, 0.0), axis=0, keepdims=True)
    for step in range(1, Y):
        pltpu.make_async_remote_copy(
            src_ref=ymom.at[y], dst_ref=ymom.at[y], send_sem=s_ymom, recv_sem=r_ymom,
            device_id={"pix": (y + step) % Y}, device_id_type=MESH,
        ).start()
    def spread(step):
        zz = (z + step) % Z
        taken(gath.at[core, x], 1, r_z.at[zz])
        chunk = (core, x, zz)
        for hop in (1, 3, 2):
            pass_on(chunk, s_x, r_x.at[zz], date_at(z, (x + hop) % X, core))
        pass_on(chunk, s_core, r_core, date_at(z, x, 1 - core))

    spread(1)
    spread(7)
    taken(ymom, Y - 1, r_ymom)
    dmom[me] = (ymom[0] + ymom[1]) + (ymom[2] + ymom[3])

    @pl.loop(1, PEERS)
    def _(step):
        to = peer(step)
        pltpu.make_async_remote_copy(
            src_ref=dmom.at[me], dst_ref=dmom.at[me], send_sem=s_dmom, recv_sem=r_dmom,
            device_id={"date": to}, device_id_type=MESH,
        ).start()

    for step in (2, 6, 3, 5, 4):
        spread(step)
    for step in (0, 1, 7, 2, 6, 3, 5, 4):
        zz = (z + step) % Z
        taken(gath.at[core, x], X - 1, r_x.at[zz])
        for hop in (1, 3, 2):
            pass_on((core, (x + hop) % X, zz), s_core, r_core, date_at(z, x, 1 - core))

    taken(dmom, PEERS - 1, r_dmom)
    total = dmom[0]
    for d in range(1, PEERS):
        total = total + dmom[d]
    lane = lax.broadcasted_iota(jnp.int32, (1, LANES), 1)
    means, scales = [], []
    for b in range(bands):
        mean = jnp.sum(jnp.where(lane == b, total, 0.0), axis=1, keepdims=True) / pixels
        second = jnp.sum(jnp.where(lane == bands + b, total, 0.0), axis=1, keepdims=True) / pixels
        var = second - mean * mean
        means.append(mean)
        scales.append(1.0 / jnp.sqrt(var + EPS))

    pltpu.make_async_copy(gath.at[0], gath.at[0], r_core).wait()

    @pl.loop(0, Z)
    def _(zz):
        for cc in range(CORE):
            tile = pl.ds(pl.multiple_of((zz * CORE + cc) * LANES, LANES), LANES)
            for b in range(bands):
                block = jnp.concatenate([gath[cc, k, zz, b] for k in range(PAIRS)], axis=0)
                out_ref[b, :, tile] = (block - means[b]) * scales[b]

    taken(send, PEERS - 1, s_stack)
    taken(vsend, PEERS - 1, s_valid)
    taken(dmom, PEERS - 1, s_dmom)
    taken(ymom, Y - 1, s_ymom)
    taken(gath.at[0, 0], Z - 1, s_z)
    taken(gath.at[0], X - 1, s_x)
    pltpu.make_async_copy(gath.at[0], gath.at[0], s_core).wait()


def body(stack, cloud):
    _, bands, rows, cols = stack.shape
    pixels = float(lax.axis_size("pix") * rows * cols)
    f32, bf16 = jnp.float32, jnp.bfloat16
    dma = pltpu.SemaphoreType.DMA
    return pl.pallas_call(
        functools.partial(kernel, pixels),
        out_shape=jax.ShapeDtypeStruct((bands, rows, cols), f32),
        in_specs=[pl.BlockSpec(memory_space=pltpu.HBM)] * 2,
        out_specs=pl.BlockSpec(memory_space=pltpu.VMEM),
        scratch_shapes=[
            pltpu.VMEM((bands, rows, cols), bf16),
            pltpu.VMEM((rows, cols), jnp.int32),
            pltpu.VMEM((PEERS, bands, 2, LANES), bf16),
            pltpu.VMEM((PEERS, bands, 2, LANES), bf16),
            pltpu.VMEM((2, 1, cols), f32),
            pltpu.VMEM((2, 1, cols), f32),
            pltpu.VMEM((PEERS, 2, LANES), bf16),
            pltpu.VMEM((PEERS, 2, LANES), bf16),
            pltpu.VMEM((2, bands, PEERS, LANES), f32),
            pltpu.VMEM((2, PEERS, LANES), f32),
            pltpu.VMEM((CORE, X, Z, bands, 2, LANES), f32),
            pltpu.VMEM((2, 2 * bands, LANES), f32),
            pltpu.VMEM((Y, 1, LANES), f32),
            pltpu.VMEM((PEERS, 1, LANES), f32),
            dma, dma((Z,)), dma((2,)), dma((2,)), dma, dma,
            dma, dma, dma, dma((Z,)), dma((Z,)), dma, dma, dma, dma, dma,
            dma((2,)),
        ],
        compiler_params=pltpu.CompilerParams(collective_id=0, has_side_effects=True, vmem_limit_bytes=8 << 20),
    )(pltpu.with_memory_space_constraint(stack[0], pltpu.HBM), pltpu.with_memory_space_constraint(cloud[0], pltpu.HBM))


def solution(mesh):
    placed = (P("date", None, "pix", None), P("date", "pix", None))
    return jax.shard_map(
        body, mesh=mesh, in_specs=placed, out_specs=P(None, "pix", None), check_vma=False
    )
```

```python
import functools

import jax
import jax.numpy as jnp
from jax import lax
from jax.experimental import pallas as pl
from jax.experimental.pallas import tpu as pltpu
from jax.sharding import PartitionSpec as P

ITERS = 2
DELTA_SQ = 0.01
EPS = 1e-05
MESH = pl.DeviceIdType.MESH
TOP = 32767.0
MID_COARSE, MID_FINE = 2.0**11, 2.0**26
POWER = 256.0
Z, X, CORE, Y = 8, 4, 2, 4
LINE = X * CORE
PEERS = Z * LINE
PAIRS = 4
LANES = 128


def kernel(
    pixels, stack_hbm, cloud_hbm, out_ref,
    stack_ref, cloud_ref, send, recv, hsend, hrecv, vsend, vrecv, work, seen, gath, med, ymom, dmom,
    s_stack, r_stack, s_halo, r_halo, s_valid, r_valid,
    s_z, s_x, s_core, r_z, r_x, r_core, s_ymom, r_ymom, s_dmom, r_dmom,
    s_in,
):
    bands = stack_ref.shape[0]
    rows, cols = cloud_ref.shape
    me = lax.axis_index("date")
    y = lax.axis_index("pix")
    z = me // (X * CORE)
    x = (me // CORE) % X
    core = me % CORE

    def date_at(zz, xx, cc):
        return (zz * X + xx) * CORE + cc

    def peer(step):
        return (me + step) % PEERS

    def in_line(zz, step):
        return zz * LINE + (me % LINE + step) % LINE

    def give(zz, first):
        @pl.loop(first, LINE)
        def _(step):
            to = in_line(zz, step)
            pltpu.make_async_remote_copy(
                src_ref=send.at[to], dst_ref=recv.at[me],
                send_sem=s_stack, recv_sem=r_stack.at[z],
                device_id={"date": to}, device_id_type=MESH,
            ).start()

    fetches = [
        pltpu.make_async_copy(cloud_hbm, cloud_ref, s_in.at[0]),
        pltpu.make_async_copy(stack_hbm, stack_ref, s_in.at[1]),
    ]

    barrier = pltpu.get_barrier_semaphore()
    for copy in fetches:
        copy.start()

    @pl.loop(1, PEERS)
    def _(step):
        pl.semaphore_signal(barrier, inc=1, device_id={"date": peer(step)}, device_id_type=MESH)

    for step in range(1, Y):
        pl.semaphore_signal(barrier, inc=1, device_id={"pix": (y + step) % Y}, device_id_type=MESH)

    for copy in fetches:
        copy.wait()

    @pl.loop(0, Z)
    def _(zz):
        for cc in range(CORE):
            tile = pl.ds(pl.multiple_of((zz * CORE + cc) * LANES, LANES), LANES)
            for k in range(PAIRS):
                send[date_at(zz, k, cc)] = stack_ref[:, 2 * k : 2 * k + 2, tile]

    recv[me] = send[me]
    cloudy = (1 - cloud_ref[...]).astype(jnp.float32)
    hsend[0] = cloudy[0:1]
    hsend[1] = cloudy[rows - 1 : rows]

    pl.semaphore_wait(barrier, PEERS - 1 + Y - 1)

    halos = []
    for side, to in ((0, (y + Y - 1) % Y), (1, (y + 1) % Y)):
        halos.append(
            pltpu.make_async_remote_copy(
                src_ref=hsend.at[side], dst_ref=hrecv.at[side],
                send_sem=s_halo.at[side], recv_sem=r_halo.at[side],
                device_id={"pix": to}, device_id_type=MESH,
            )
        )
    for copy in halos:
        copy.start()

    for dz in (4, 3, 5, 2, 6, 1, 7):
        give((z + dz) % Z, 0)
    give(z, 1)

    for copy in halos:
        copy.wait()
    above = jnp.where(y > 0, hrecv[1], 0.0)
    below = jnp.where(y < Y - 1, hrecv[0], 0.0)
    row = lax.broadcasted_iota(jnp.int32, (rows, cols), 0)
    col = lax.broadcasted_iota(jnp.int32, (rows, cols), 1)
    near = jnp.maximum(cloudy, jnp.where(row == 0, above, pltpu.roll(cloudy, 1, 0)))
    near = jnp.maximum(near, jnp.where(row == rows - 1, below, pltpu.roll(cloudy, rows - 1, 0)))
    near = jnp.maximum(near, jnp.where(col == 0, 0.0, pltpu.roll(cloudy, 1, 1)))
    near = jnp.maximum(near, jnp.where(col == cols - 1, 0.0, pltpu.roll(cloudy, cols - 1, 1)))
    valid = 1.0 - near
    for c in range(Z * CORE):
        for k in range(PAIRS):
            block = valid[2 * k : 2 * k + 2, c * LANES : (c + 1) * LANES]
            vsend[date_at(c // CORE, k, c % CORE)] = block.astype(jnp.bfloat16)
    vrecv[me] = vsend[me]

    @pl.loop(1, PEERS)
    def _(step):
        to = peer(step)
        pltpu.make_async_remote_copy(
            src_ref=vsend.at[to], dst_ref=vrecv.at[me], send_sem=s_valid, recv_sem=r_valid,
            device_id={"date": to}, device_id_type=MESH,
        ).start()

    def taken(ref, count, sem):
        some = ref.at[pl.ds(0, count)]
        pltpu.make_async_copy(some, some, sem).wait()

    def unpack(zz):
        @pl.loop(0, LINE)
        def _(step):
            date = zz * LINE + step
            block = recv[date].astype(jnp.float32)
            for b in range(bands):
                for r in range(2):
                    work[r, b, pl.ds(date, 1), :] = block[b, r : r + 1]

    taken(recv, LINE - 1, r_stack.at[z])
    unpack(z)

    @pl.loop(1, Z)
    def _(step):
        zz = (z + step) % Z
        taken(recv, LINE, r_stack.at[zz])
        unpack(zz)

    taken(vrecv, PEERS - 1, r_valid)

    @pl.loop(0, PEERS)
    def _(date):
        block = vrecv[date].astype(jnp.float32)
        for r in range(2):
            seen[r, pl.ds(date, 1), :] = block[r : r + 1]

    @pl.loop(0, 2)
    def _(r):
        median = [jnp.zeros((1, LANES), jnp.float32)] * bands
        for step in range(ITERS + 1):
            numer = [jnp.zeros((8, LANES), jnp.float32)] * bands
            denom = jnp.zeros((8, LANES), jnp.float32)
            for j in range(0, PEERS, 8):
                values = [work[r, b, j : j + 8, :] for b in range(bands)]
                weight = seen[r, j : j + 8, :]
                if step > 0:
                    square = DELTA_SQ
                    for b in range(bands):
                        diff = values[b] - median[b]
                        square = square + diff * diff
                    weight = weight * lax.rsqrt(square)
                denom = denom + weight
                numer = [n + weight * v for n, v in zip(numer, values)]
            scale = 1.0 / (jnp.sum(denom, axis=0, keepdims=True) + 1.0)
            median = [
                (jnp.sum(n, axis=0, keepdims=True) + m) * scale for n, m in zip(numer, median)
            ]
        for b in range(bands):
            med[r, b : b + 1, :] = median[b]

    first, second = med[0], med[1]
    lane = lax.broadcasted_iota(jnp.int32, (bands, LANES), 1)
    band = lax.broadcasted_iota(jnp.int32, (bands, LANES), 0)

    def in_row(*columns):
        spread_out = jnp.zeros((bands, LANES), jnp.float32)
        for n, column in enumerate(columns):
            spread_out = jnp.where(lane == band + n * bands, column, spread_out)
        return jnp.sum(spread_out, axis=0, keepdims=True)

    ymom[y] = in_row(
        jnp.sum(first + second, axis=1, keepdims=True),
        jnp.sum(first * first + second * second, axis=1, keepdims=True),
    )
    for step in range(1, Y):
        pltpu.make_async_remote_copy(
            src_ref=ymom.at[y], dst_ref=ymom.at[y], send_sem=s_ymom, recv_sem=r_ymom,
            device_id={"pix": (y + step) % Y}, device_id_type=MESH,
        ).start()

    high = jnp.max(jnp.maximum(first, second), axis=1, keepdims=True)
    low = jnp.min(jnp.minimum(first, second), axis=1, keepdims=True)
    middle = 0.5 * (high + low)
    coarse = jnp.round(middle * MID_COARSE)
    fine = jnp.round((middle - coarse / MID_COARSE) * MID_FINE)
    middle = coarse / MID_COARSE + fine / MID_FINE
    reach = jnp.maximum(jnp.maximum(high - middle, middle - low), 2.0**-60)
    power = jnp.ceil(jnp.log2(reach) * POWER) + 1.0
    to_code = jnp.exp2(power * (-1.0 / POWER)) * TOP
    codes = [
        jnp.clip(jnp.round((rows_of - middle) * to_code), -TOP, TOP).astype(jnp.int32)
        for rows_of in (first, second)
    ]
    for b in range(bands):
        pair = jnp.concatenate([codes[0][b : b + 1], codes[1][b : b + 1]], axis=0)
        gath[core, x, z, b] = pair.astype(jnp.int16)
    header = in_row(coarse, fine, power).astype(jnp.int32)
    gath[core, x, z, bands] = jnp.concatenate([header, header], axis=0).astype(jnp.int16)

    def pass_on(chunk, send_sem, recv_sem, to):
        pltpu.make_async_remote_copy(
            src_ref=gath.at[chunk], dst_ref=gath.at[chunk],
            send_sem=send_sem, recv_sem=recv_sem,
            device_id={"date": to}, device_id_type=MESH,
        ).start()

    for step in (1, 7, 2, 6, 3, 5, 4):
        pass_on((core, x, z), s_z, r_z.at[z], date_at((z + step) % Z, x, core))
    for step in (1, 3, 2):
        pass_on((core, x, z), s_x, r_x.at[z], date_at(z, (x + step) % X, core))
    pass_on((core, x, z), s_core, r_core.at[z], date_at(z, x, 1 - core))

    def spread(step):
        zz = (z + step) % Z
        taken(gath.at[core, x], 1, r_z.at[zz])
        chunk = (core, x, zz)
        for hop in (1, 3, 2):
            pass_on(chunk, s_x, r_x.at[zz], date_at(z, (x + hop) % X, core))
        pass_on(chunk, s_core, r_core.at[zz], date_at(z, x, 1 - core))

    spread(1)
    spread(7)
    taken(ymom, Y - 1, r_ymom)
    dmom[me] = (ymom[0] + ymom[1]) + (ymom[2] + ymom[3])

    @pl.loop(1, PEERS)
    def _(step):
        to = peer(step)
        pltpu.make_async_remote_copy(
            src_ref=dmom.at[me], dst_ref=dmom.at[me], send_sem=s_dmom, recv_sem=r_dmom,
            device_id={"date": to}, device_id_type=MESH,
        ).start()

    for step in (2, 6, 3, 5, 4):
        spread(step)
    def tile_of(cc, zz):
        return pl.ds(pl.multiple_of((zz * CORE + cc) * LANES, LANES), LANES)

    def decode(cc, zz):
        for b in range(bands):
            pairs = [gath[cc, k, zz, b].astype(jnp.int32) for k in range(PAIRS)]
            out_ref[b, :, tile_of(cc, zz)] = jnp.concatenate(pairs, axis=0).astype(jnp.float32)

    for step in (0, 1, 7, 2, 6, 3, 5, 4):
        zz = (z + step) % Z
        taken(gath.at[core, x], X - 1, r_x.at[zz])
        for hop in (1, 3, 2):
            pass_on((core, (x + hop) % X, zz), s_core, r_core.at[zz], date_at(z, x, 1 - core))
        decode(core, zz)

    taken(dmom, PEERS - 1, r_dmom)
    total = dmom[0]
    for d in range(1, PEERS):
        total = total + dmom[d]
    mean = total / pixels
    var = pltpu.roll(mean, LANES - bands, 1) - mean * mean
    scale = 1.0 / jnp.sqrt(var + EPS)

    def finish(cc, zz):
        ranges = jnp.concatenate(
            [gath[cc, k, zz, bands].astype(jnp.int32) for k in range(PAIRS)], axis=0
        ).astype(jnp.float32)
        fines = pltpu.roll(ranges, LANES - bands, 1)
        powers = pltpu.roll(ranges, LANES - 2 * bands, 1)
        middles = ranges / MID_COARSE + fines / MID_FINE
        gain = jnp.exp2(powers * (1.0 / POWER)) * (1.0 / TOP) * scale
        shift = (middles - mean) * scale
        for b in range(bands):
            block = out_ref[b, :, tile_of(cc, zz)]
            out_ref[b, :, tile_of(cc, zz)] = block * gain[:, b : b + 1] + shift[:, b : b + 1]

    for step in (0, 1, 7, 2, 6, 3, 5, 4):
        finish(core, (z + step) % Z)
    for step in (0, 1, 7, 2, 6, 3, 5, 4):
        zz = (z + step) % Z
        taken(gath.at[0, 0], X, r_core.at[zz])
        decode(1 - core, zz)
        finish(1 - core, zz)

    taken(send, PEERS - 1, s_stack)
    taken(vsend, PEERS - 1, s_valid)
    taken(dmom, PEERS - 1, s_dmom)
    taken(ymom, Y - 1, s_ymom)
    taken(gath.at[0, 0], Z - 1, s_z)
    taken(gath.at[0], X - 1, s_x)
    pltpu.make_async_copy(gath.at[0], gath.at[0], s_core).wait()


def body(stack, cloud):
    _, bands, rows, cols = stack.shape
    pixels = float(lax.axis_size("pix") * rows * cols)
    f32, bf16 = jnp.float32, jnp.bfloat16
    dma = pltpu.SemaphoreType.DMA
    return pl.pallas_call(
        functools.partial(kernel, pixels),
        out_shape=jax.ShapeDtypeStruct((bands, rows, cols), f32),
        in_specs=[pl.BlockSpec(memory_space=pltpu.HBM)] * 2,
        out_specs=pl.BlockSpec(memory_space=pltpu.VMEM),
        scratch_shapes=[
            pltpu.VMEM((bands, rows, cols), bf16),
            pltpu.VMEM((rows, cols), jnp.int32),
            pltpu.VMEM((PEERS, bands, 2, LANES), bf16),
            pltpu.VMEM((PEERS, bands, 2, LANES), bf16),
            pltpu.VMEM((2, 1, cols), f32),
            pltpu.VMEM((2, 1, cols), f32),
            pltpu.VMEM((PEERS, 2, LANES), bf16),
            pltpu.VMEM((PEERS, 2, LANES), bf16),
            pltpu.VMEM((2, bands, PEERS, LANES), f32),
            pltpu.VMEM((2, PEERS, LANES), f32),
            pltpu.VMEM((CORE, X, Z, bands + 1, 2, LANES), jnp.int16),
            pltpu.VMEM((2, bands, LANES), f32),
            pltpu.VMEM((Y, 1, LANES), f32),
            pltpu.VMEM((PEERS, 1, LANES), f32),
            dma, dma((Z,)), dma((2,)), dma((2,)), dma, dma,
            dma, dma, dma, dma((Z,)), dma((Z,)), dma((Z,)), dma, dma, dma, dma,
            dma((2,)),
        ],
        compiler_params=pltpu.CompilerParams(collective_id=0, has_side_effects=True, vmem_limit_bytes=8 << 20),
    )(pltpu.with_memory_space_constraint(stack[0], pltpu.HBM), pltpu.with_memory_space_constraint(cloud[0], pltpu.HBM))


def solution(mesh):
    placed = (P("date", None, "pix", None), P("date", "pix", None))
    return jax.shard_map(
        body, mesh=mesh, in_specs=placed, out_specs=P(None, "pix", None), check_vma=False
    )
```

```python
import functools

import jax
import jax.numpy as jnp
from jax import lax
from jax.experimental import pallas as pl
from jax.experimental.pallas import tpu as pltpu
from jax.sharding import PartitionSpec as P

ITERS = 2
DELTA_SQ = 0.01
EPS = 1e-05
MESH = pl.DeviceIdType.MESH
Z, X, CORE, Y = 8, 4, 2, 4
LINE = X * CORE
PEERS = Z * LINE
PAIRS = 4
LANES = 128


def kernel(
    pixels, stack_hbm, cloud_hbm, out_ref,
    stack_ref, cloud_ref, send, recv, hsend, hrecv, vsend, vrecv, work, seen, gath, part, ymom, dmom,
    s_stack, r_stack, s_halo, r_halo, s_valid, r_valid,
    s_z, s_x, s_core, r_z, r_x, r_core, s_ymom, r_ymom, s_dmom, r_dmom,
    s_in, far,
):
    bands = stack_ref.shape[0]
    rows, cols = cloud_ref.shape
    me = lax.axis_index("date")
    y = lax.axis_index("pix")
    z = me // (X * CORE)
    x = (me // CORE) % X
    core = me % CORE

    def date_at(zz, xx, cc):
        return (zz * X + xx) * CORE + cc

    def peer(step):
        return (me + step) % PEERS

    def in_line(zz, step):
        return zz * LINE + (me % LINE + step) % LINE

    def give(zz, first):
        @pl.loop(first, LINE)
        def _(step):
            to = in_line(zz, step)
            pltpu.make_async_remote_copy(
                src_ref=send.at[to], dst_ref=recv.at[me],
                send_sem=s_stack, recv_sem=r_stack.at[z],
                device_id={"date": to}, device_id_type=MESH,
            ).start()

    fetches = [
        pltpu.make_async_copy(cloud_hbm, cloud_ref, s_in.at[0]),
        pltpu.make_async_copy(stack_hbm, stack_ref, s_in.at[1]),
    ]

    barrier = pltpu.get_barrier_semaphore()
    for copy in fetches:
        copy.start()

    def greet(zz, first):
        @pl.loop(first, LINE)
        def _(step):
            pl.semaphore_signal(
                barrier, inc=1, device_id={"date": in_line(zz, step)}, device_id_type=MESH
            )

    for dz in (2, 6, 1, 7):
        greet((z + dz) % Z, 0)
    greet(z, 1)

    for step in range(1, Y):
        pl.semaphore_signal(barrier, inc=1, device_id={"pix": (y + step) % Y}, device_id_type=MESH)

    for copy in fetches:
        copy.wait()

    @pl.loop(0, Z)
    def _(zz):
        for cc in range(CORE):
            tile = pl.ds(pl.multiple_of((zz * CORE + cc) * LANES, LANES), LANES)
            for k in range(PAIRS):
                send[date_at(zz, k, cc)] = stack_ref[:, 2 * k : 2 * k + 2, tile]

    recv[me] = send[me]
    cloudy = (1 - cloud_ref[...]).astype(jnp.float32)
    hsend[0] = cloudy[0:1]
    hsend[1] = cloudy[rows - 1 : rows]

    pl.semaphore_wait(barrier, 5 * LINE - 1 + Y - 1)
    for slot, dz in enumerate((Z - 1, 1, Z - 2)):
        to = date_at((z + dz) % Z, x, core)
        pl.semaphore_signal(far.at[slot], inc=1, device_id={"date": to}, device_id_type=MESH)

    halos = []
    for side, to in ((0, (y + Y - 1) % Y), (1, (y + 1) % Y)):
        halos.append(
            pltpu.make_async_remote_copy(
                src_ref=hsend.at[side], dst_ref=hrecv.at[side],
                send_sem=s_halo.at[side], recv_sem=r_halo.at[side],
                device_id={"pix": to}, device_id_type=MESH,
            )
        )
    for copy in halos:
        copy.start()

    for dz in (2, 6, 1, 7):
        give((z + dz) % Z, 0)
    give(z, 1)
    for slot, dz in enumerate((3, 5, 4)):
        pl.semaphore_wait(far.at[slot], 1)
        give((z + dz) % Z, 0)

    for copy in halos:
        copy.wait()
    above = jnp.where(y > 0, hrecv[1], 0.0)
    below = jnp.where(y < Y - 1, hrecv[0], 0.0)
    row = lax.broadcasted_iota(jnp.int32, (rows, cols), 0)
    col = lax.broadcasted_iota(jnp.int32, (rows, cols), 1)
    near = jnp.maximum(cloudy, jnp.where(row == 0, above, pltpu.roll(cloudy, 1, 0)))
    near = jnp.maximum(near, jnp.where(row == rows - 1, below, pltpu.roll(cloudy, rows - 1, 0)))
    near = jnp.maximum(near, jnp.where(col == 0, 0.0, pltpu.roll(cloudy, 1, 1)))
    near = jnp.maximum(near, jnp.where(col == cols - 1, 0.0, pltpu.roll(cloudy, cols - 1, 1)))
    valid = 1.0 - near
    for c in range(Z * CORE):
        for k in range(PAIRS):
            block = valid[2 * k : 2 * k + 2, c * LANES : (c + 1) * LANES]
            vsend[date_at(c // CORE, k, c % CORE)] = block.astype(jnp.bfloat16)
    vrecv[me] = vsend[me]

    @pl.loop(1, PEERS)
    def _(step):
        to = peer(step)
        pltpu.make_async_remote_copy(
            src_ref=vsend.at[to], dst_ref=vrecv.at[me], send_sem=s_valid, recv_sem=r_valid,
            device_id={"date": to}, device_id_type=MESH,
        ).start()

    def taken(ref, count, sem):
        some = ref.at[pl.ds(0, count)]
        pltpu.make_async_copy(some, some, sem).wait()

    def unpack(zz):
        @pl.loop(0, LINE)
        def _(step):
            date = zz * LINE + step
            block = recv[date].astype(jnp.float32)
            for b in range(bands):
                for r in range(2):
                    work[r, b, pl.ds(date, 1), :] = block[b, r : r + 1]

    taken(recv, LINE - 1, r_stack.at[z])
    unpack(z)

    @pl.loop(1, Z)
    def _(step):
        zz = (z + step) % Z
        taken(recv, LINE, r_stack.at[zz])
        unpack(zz)

    taken(vrecv, PEERS - 1, r_valid)

    @pl.loop(0, PEERS)
    def _(date):
        block = vrecv[date].astype(jnp.float32)
        for r in range(2):
            seen[r, pl.ds(date, 1), :] = block[r : r + 1]

    @pl.loop(0, 2)
    def _(r):
        median = [jnp.zeros((1, LANES), jnp.float32)] * bands
        for step in range(ITERS + 1):
            numer = [jnp.zeros((8, LANES), jnp.float32)] * bands
            denom = jnp.zeros((8, LANES), jnp.float32)
            for j in range(0, PEERS, 8):
                values = [work[r, b, j : j + 8, :] for b in range(bands)]
                weight = seen[r, j : j + 8, :]
                if step > 0:
                    square = DELTA_SQ
                    for b in range(bands):
                        diff = values[b] - median[b]
                        square = square + diff * diff
                    weight = weight * lax.rsqrt(square)
                denom = denom + weight
                numer = [n + weight * v for n, v in zip(numer, values)]
            scale = 1.0 / (jnp.sum(denom, axis=0, keepdims=True) + 1.0)
            median = [
                (jnp.sum(n, axis=0, keepdims=True) + m) * scale for n, m in zip(numer, median)
            ]
        for b in range(bands):
            gath[core, x, z, b, pl.ds(r, 1), :] = median[b]
            part[r, b : b + 1, :] = median[b]
            part[r, bands + b : bands + b + 1, :] = median[b] * median[b]

    def pass_on(chunk, send_sem, recv_sem, to):
        pltpu.make_async_remote_copy(
            src_ref=gath.at[chunk], dst_ref=gath.at[chunk],
            send_sem=send_sem, recv_sem=recv_sem,
            device_id={"date": to}, device_id_type=MESH,
        ).start()

    for step in (1, 7, 2, 6, 3, 5, 4):
        pass_on((core, x, z), s_z, r_z.at[z], date_at((z + step) % Z, x, core))
    for step in (1, 3, 2):
        pass_on((core, x, z), s_x, r_x.at[z], date_at(z, (x + step) % X, core))
    pass_on((core, x, z), s_core, r_core, date_at(z, x, 1 - core))

    sums = jnp.sum(part[0] + part[1], axis=1, keepdims=True)
    lane = lax.broadcasted_iota(jnp.int32, (2 * bands, LANES), 1)
    which = lax.broadcasted_iota(jnp.int32, (2 * bands, LANES), 0)
    ymom[y] = jnp.sum(jnp.where(lane == which, sums, 0.0), axis=0, keepdims=True)
    for step in range(1, Y):
        pltpu.make_async_remote_copy(
            src_ref=ymom.at[y], dst_ref=ymom.at[y], send_sem=s_ymom, recv_sem=r_ymom,
            device_id={"pix": (y + step) % Y}, device_id_type=MESH,
        ).start()
    def spread(step):
        zz = (z + step) % Z
        taken(gath.at[core, x], 1, r_z.at[zz])
        chunk = (core, x, zz)
        for hop in (1, 3, 2):
            pass_on(chunk, s_x, r_x.at[zz], date_at(z, (x + hop) % X, core))
        pass_on(chunk, s_core, r_core, date_at(z, x, 1 - core))

    spread(1)
    spread(7)
    taken(ymom, Y - 1, r_ymom)
    dmom[me] = (ymom[0] + ymom[1]) + (ymom[2] + ymom[3])

    @pl.loop(1, PEERS)
    def _(step):
        to = peer(step)
        pltpu.make_async_remote_copy(
            src_ref=dmom.at[me], dst_ref=dmom.at[me], send_sem=s_dmom, recv_sem=r_dmom,
            device_id={"date": to}, device_id_type=MESH,
        ).start()

    for step in (2, 6, 3, 5, 4):
        spread(step)
    for step in (0, 1, 7, 2, 6, 3, 5, 4):
        zz = (z + step) % Z
        taken(gath.at[core, x], X - 1, r_x.at[zz])
        for hop in (1, 3, 2):
            pass_on((core, (x + hop) % X, zz), s_core, r_core, date_at(z, x, 1 - core))

    taken(dmom, PEERS - 1, r_dmom)
    total = dmom[0]
    for d in range(1, PEERS):
        total = total + dmom[d]
    lane = lax.broadcasted_iota(jnp.int32, (1, LANES), 1)
    means, scales = [], []
    for b in range(bands):
        mean = jnp.sum(jnp.where(lane == b, total, 0.0), axis=1, keepdims=True) / pixels
        second = jnp.sum(jnp.where(lane == bands + b, total, 0.0), axis=1, keepdims=True) / pixels
        var = second - mean * mean
        means.append(mean)
        scales.append(1.0 / jnp.sqrt(var + EPS))

    pltpu.make_async_copy(gath.at[0], gath.at[0], r_core).wait()

    @pl.loop(0, Z)
    def _(zz):
        for cc in range(CORE):
            tile = pl.ds(pl.multiple_of((zz * CORE + cc) * LANES, LANES), LANES)
            for b in range(bands):
                block = jnp.concatenate([gath[cc, k, zz, b] for k in range(PAIRS)], axis=0)
                out_ref[b, :, tile] = (block - means[b]) * scales[b]

    taken(send, PEERS - 1, s_stack)
    taken(vsend, PEERS - 1, s_valid)
    taken(dmom, PEERS - 1, s_dmom)
    taken(ymom, Y - 1, s_ymom)
    taken(gath.at[0, 0], Z - 1, s_z)
    taken(gath.at[0], X - 1, s_x)
    pltpu.make_async_copy(gath.at[0], gath.at[0], s_core).wait()


def body(stack, cloud):
    _, bands, rows, cols = stack.shape
    pixels = float(lax.axis_size("pix") * rows * cols)
    f32, bf16 = jnp.float32, jnp.bfloat16
    dma = pltpu.SemaphoreType.DMA
    return pl.pallas_call(
        functools.partial(kernel, pixels),
        out_shape=jax.ShapeDtypeStruct((bands, rows, cols), f32),
        in_specs=[pl.BlockSpec(memory_space=pltpu.HBM)] * 2,
        out_specs=pl.BlockSpec(memory_space=pltpu.VMEM),
        scratch_shapes=[
            pltpu.VMEM((bands, rows, cols), bf16),
            pltpu.VMEM((rows, cols), jnp.int32),
            pltpu.VMEM((PEERS, bands, 2, LANES), bf16),
            pltpu.VMEM((PEERS, bands, 2, LANES), bf16),
            pltpu.VMEM((2, 1, cols), f32),
            pltpu.VMEM((2, 1, cols), f32),
            pltpu.VMEM((PEERS, 2, LANES), bf16),
            pltpu.VMEM((PEERS, 2, LANES), bf16),
            pltpu.VMEM((2, bands, PEERS, LANES), f32),
            pltpu.VMEM((2, PEERS, LANES), f32),
            pltpu.VMEM((CORE, X, Z, bands, 2, LANES), f32),
            pltpu.VMEM((2, 2 * bands, LANES), f32),
            pltpu.VMEM((Y, 1, LANES), f32),
            pltpu.VMEM((PEERS, 1, LANES), f32),
            dma, dma((Z,)), dma((2,)), dma((2,)), dma, dma,
            dma, dma, dma, dma((Z,)), dma((Z,)), dma, dma, dma, dma, dma,
            dma((2,)), pltpu.SemaphoreType.REGULAR((3,)),
        ],
        compiler_params=pltpu.CompilerParams(collective_id=0, has_side_effects=True, vmem_limit_bytes=8 << 20),
    )(pltpu.with_memory_space_constraint(stack[0], pltpu.HBM), pltpu.with_memory_space_constraint(cloud[0], pltpu.HBM))


def solution(mesh):
    placed = (P("date", None, "pix", None), P("date", "pix", None))
    return jax.shard_map(
        body, mesh=mesh, in_specs=placed, out_specs=P(None, "pix", None), check_vma=False
    )
```

```python
import functools

import jax
import jax.numpy as jnp
from jax import lax
from jax.experimental import pallas as pl
from jax.experimental.pallas import tpu as pltpu
from jax.sharding import PartitionSpec as P

ITERS = 2
DELTA_SQ = 0.01
EPS = 1e-05
MESH = pl.DeviceIdType.MESH
Z, X, CORE, Y = 8, 4, 2, 4
LINE = X * CORE
PEERS = Z * LINE
PAIRS = 4
LANES = 128


def kernel(
    pixels, stack_hbm, cloud_hbm, out_ref,
    stack_ref, cloud_ref, send, recv, hsend, hrecv, vsend, vrecv, work, seen, gath, part, ymom, dmom,
    s_stack, r_stack, s_halo, r_halo, s_valid, r_valid,
    s_z, s_x, s_core, r_z, r_x, r_core, s_ymom, r_ymom, s_dmom, r_dmom,
    s_in, far,
):
    bands = stack_ref.shape[0]
    rows, cols = cloud_ref.shape
    me = lax.axis_index("date")
    y = lax.axis_index("pix")
    z = me // (X * CORE)
    x = (me // CORE) % X
    core = me % CORE

    def date_at(zz, xx, cc):
        return (zz * X + xx) * CORE + cc

    def peer(step):
        return (me + step) % PEERS

    def in_line(zz, step):
        return zz * LINE + (me % LINE + step) % LINE

    def give(zz, first):
        @pl.loop(first, LINE)
        def _(step):
            to = in_line(zz, step)
            pltpu.make_async_remote_copy(
                src_ref=send.at[to], dst_ref=recv.at[me],
                send_sem=s_stack, recv_sem=r_stack.at[z],
                device_id={"date": to}, device_id_type=MESH,
            ).start()

    fetches = [
        pltpu.make_async_copy(cloud_hbm, cloud_ref, s_in.at[0]),
        pltpu.make_async_copy(stack_hbm, stack_ref, s_in.at[1]),
    ]

    barrier = pltpu.get_barrier_semaphore()
    for copy in fetches:
        copy.start()

    def greet(zz, first):
        @pl.loop(first, LINE)
        def _(step):
            pl.semaphore_signal(
                barrier, inc=1, device_id={"date": in_line(zz, step)}, device_id_type=MESH
            )

    for dz in (2, 6, 1, 7):
        greet((z + dz) % Z, 0)
    greet(z, 1)

    for step in range(1, Y):
        pl.semaphore_signal(barrier, inc=1, device_id={"pix": (y + step) % Y}, device_id_type=MESH)

    for copy in fetches:
        copy.wait()

    @pl.loop(0, Z)
    def _(zz):
        for cc in range(CORE):
            tile = pl.ds(pl.multiple_of((zz * CORE + cc) * LANES, LANES), LANES)
            for k in range(PAIRS):
                send[date_at(zz, k, cc)] = stack_ref[:, 2 * k : 2 * k + 2, tile]

    recv[me] = send[me]
    cloudy = (1 - cloud_ref[...]).astype(jnp.float32)
    hsend[0] = cloudy[0:1]
    hsend[1] = cloudy[rows - 1 : rows]

    pl.semaphore_wait(barrier, 5 * LINE - 1 + Y - 1)
    for slot, dz in enumerate((Z - 1, 1, Z - 2)):
        to = date_at((z + dz) % Z, x, core)
        pl.semaphore_signal(far.at[slot], inc=1, device_id={"date": to}, device_id_type=MESH)

    halos = []
    for side, to in ((0, (y + Y - 1) % Y), (1, (y + 1) % Y)):
        halos.append(
            pltpu.make_async_remote_copy(
                src_ref=hsend.at[side], dst_ref=hrecv.at[side],
                send_sem=s_halo.at[side], recv_sem=r_halo.at[side],
                device_id={"pix": to}, device_id_type=MESH,
            )
        )
    for copy in halos:
        copy.start()

    for dz in (2, 6, 1, 7):
        give((z + dz) % Z, 0)
    give(z, 1)
    for slot, dz in enumerate((3, 5, 4)):
        pl.semaphore_wait(far.at[slot], 1)
        give((z + dz) % Z, 0)

    for copy in halos:
        copy.wait()
    above = jnp.where(y > 0, hrecv[1], 0.0)
    below = jnp.where(y < Y - 1, hrecv[0], 0.0)
    row = lax.broadcasted_iota(jnp.int32, (rows, cols), 0)
    col = lax.broadcasted_iota(jnp.int32, (rows, cols), 1)
    near = jnp.maximum(cloudy, jnp.where(row == 0, above, pltpu.roll(cloudy, 1, 0)))
    near = jnp.maximum(near, jnp.where(row == rows - 1, below, pltpu.roll(cloudy, rows - 1, 0)))
    near = jnp.maximum(near, jnp.where(col == 0, 0.0, pltpu.roll(cloudy, 1, 1)))
    near = jnp.maximum(near, jnp.where(col == cols - 1, 0.0, pltpu.roll(cloudy, cols - 1, 1)))
    valid = 1.0 - near
    for c in range(Z * CORE):
        for k in range(PAIRS):
            block = valid[2 * k : 2 * k + 2, c * LANES : (c + 1) * LANES]
            vsend[date_at(c // CORE, k, c % CORE)] = block.astype(jnp.bfloat16)
    vrecv[me] = vsend[me]

    @pl.loop(1, PEERS)
    def _(step):
        to = peer(step)
        pltpu.make_async_remote_copy(
            src_ref=vsend.at[to], dst_ref=vrecv.at[me], send_sem=s_valid, recv_sem=r_valid,
            device_id={"date": to}, device_id_type=MESH,
        ).start()

    def taken(ref, count, sem):
        some = ref.at[pl.ds(0, count)]
        pltpu.make_async_copy(some, some, sem).wait()

    def unpack(zz):
        @pl.loop(0, LINE, unroll=True)
        def _(step):
            date = zz * LINE + step
            block = recv[date].astype(jnp.float32)
            for b in range(bands):
                for r in range(2):
                    work[r, b, pl.ds(date, 1), :] = block[b, r : r + 1]

    taken(recv, LINE - 1, r_stack.at[z])
    unpack(z)

    @pl.loop(1, Z)
    def _(step):
        zz = (z + step) % Z
        taken(recv, LINE, r_stack.at[zz])
        unpack(zz)

    taken(vrecv, PEERS - 1, r_valid)

    @pl.loop(0, PEERS, unroll=8)
    def _(date):
        block = vrecv[date].astype(jnp.float32)
        for r in range(2):
            seen[r, pl.ds(date, 1), :] = block[r : r + 1]

    medians = [[jnp.zeros((1, LANES), jnp.float32)] * bands for _ in range(2)]
    for step in range(ITERS + 1):
        for r in range(2):
            median = medians[r]
            numer = [jnp.zeros((8, LANES), jnp.float32)] * bands
            denom = jnp.zeros((8, LANES), jnp.float32)
            for j in range(0, PEERS, 8):
                values = [work[r, b, j : j + 8, :] for b in range(bands)]
                weight = seen[r, j : j + 8, :]
                if step > 0:
                    square = DELTA_SQ
                    for b in range(bands):
                        diff = values[b] - median[b]
                        square = square + diff * diff
                    weight = weight * lax.rsqrt(square)
                denom = denom + weight
                numer = [n + weight * v for n, v in zip(numer, values)]
            scale = 1.0 / (jnp.sum(denom, axis=0, keepdims=True) + 1.0)
            medians[r] = [
                (jnp.sum(n, axis=0, keepdims=True) + m) * scale for n, m in zip(numer, median)
            ]
    for r in range(2):
        for b in range(bands):
            median = medians[r][b]
            gath[core, x, z, b, r : r + 1, :] = median
            part[r, b : b + 1, :] = median
            part[r, bands + b : bands + b + 1, :] = median * median

    def pass_on(chunk, send_sem, recv_sem, to):
        pltpu.make_async_remote_copy(
            src_ref=gath.at[chunk], dst_ref=gath.at[chunk],
            send_sem=send_sem, recv_sem=recv_sem,
            device_id={"date": to}, device_id_type=MESH,
        ).start()

    for zz in (0, 1, 7, 2, 6, 3, 5, 4):

        @pl.when(zz != z)
        def _():
            pass_on((core, x, z), s_z, r_z.at[z], date_at(zz, x, core))

    def along_x(zz):
        for xx in (0, 1, 3, 2):

            @pl.when(xx != x)
            def _():
                pass_on((core, x, zz), s_x, r_x.at[zz], date_at(z, xx, core))

    along_x(z)
    pass_on((core, x, z), s_core, r_core, date_at(z, x, 1 - core))

    sums = jnp.sum(part[0] + part[1], axis=1, keepdims=True)
    lane = lax.broadcasted_iota(jnp.int32, (2 * bands, LANES), 1)
    which = lax.broadcasted_iota(jnp.int32, (2 * bands, LANES), 0)
    ymom[y] = jnp.sum(jnp.where(lane == which, sums, 0.0), axis=0, keepdims=True)
    for step in range(1, Y):
        pltpu.make_async_remote_copy(
            src_ref=ymom.at[y], dst_ref=ymom.at[y], send_sem=s_ymom, recv_sem=r_ymom,
            device_id={"pix": (y + step) % Y}, device_id_type=MESH,
        ).start()
    def spread(step):
        zz = (z + step) % Z
        taken(gath.at[core, x], 1, r_z.at[zz])
        chunk = (core, x, zz)
        along_x(zz)
        pass_on(chunk, s_core, r_core, date_at(z, x, 1 - core))

    spread(1)
    spread(7)
    taken(ymom, Y - 1, r_ymom)
    dmom[me] = (ymom[0] + ymom[1]) + (ymom[2] + ymom[3])

    @pl.loop(0, PEERS)
    def _(to):
        @pl.when(to != me)
        def _():
            pltpu.make_async_remote_copy(
                src_ref=dmom.at[me], dst_ref=dmom.at[me], send_sem=s_dmom, recv_sem=r_dmom,
                device_id={"date": to}, device_id_type=MESH,
            ).start()

    for step in (2, 6, 3, 5, 4):
        spread(step)
    for step in (0, 1, 7, 2, 6, 3, 5, 4):
        zz = (z + step) % Z
        taken(gath.at[core, x], X - 1, r_x.at[zz])
        for hop in (1, 3, 2):
            pass_on((core, (x + hop) % X, zz), s_core, r_core, date_at(z, x, 1 - core))

    taken(dmom, PEERS - 1, r_dmom)
    total = dmom[0]
    for d in range(1, PEERS):
        total = total + dmom[d]
    lane = lax.broadcasted_iota(jnp.int32, (1, LANES), 1)
    means, scales = [], []
    for b in range(bands):
        mean = jnp.sum(jnp.where(lane == b, total, 0.0), axis=1, keepdims=True) / pixels
        second = jnp.sum(jnp.where(lane == bands + b, total, 0.0), axis=1, keepdims=True) / pixels
        var = second - mean * mean
        means.append(mean)
        scales.append(1.0 / jnp.sqrt(var + EPS))

    pltpu.make_async_copy(gath.at[0], gath.at[0], r_core).wait()

    @pl.loop(0, Z)
    def _(zz):
        for cc in range(CORE):
            tile = pl.ds(pl.multiple_of((zz * CORE + cc) * LANES, LANES), LANES)
            for b in range(bands):
                block = jnp.concatenate([gath[cc, k, zz, b] for k in range(PAIRS)], axis=0)
                out_ref[b, :, tile] = (block - means[b]) * scales[b]

    taken(send, PEERS - 1, s_stack)
    taken(vsend, PEERS - 1, s_valid)
    taken(dmom, PEERS - 1, s_dmom)
    taken(ymom, Y - 1, s_ymom)
    taken(gath.at[0, 0], Z - 1, s_z)
    taken(gath.at[0], X - 1, s_x)
    pltpu.make_async_copy(gath.at[0], gath.at[0], s_core).wait()


def body(stack, cloud):
    _, bands, rows, cols = stack.shape
    pixels = float(lax.axis_size("pix") * rows * cols)
    f32, bf16 = jnp.float32, jnp.bfloat16
    dma = pltpu.SemaphoreType.DMA
    return pl.pallas_call(
        functools.partial(kernel, pixels),
        out_shape=jax.ShapeDtypeStruct((bands, rows, cols), f32),
        in_specs=[pl.BlockSpec(memory_space=pltpu.HBM)] * 2,
        out_specs=pl.BlockSpec(memory_space=pltpu.VMEM),
        scratch_shapes=[
            pltpu.VMEM((bands, rows, cols), bf16),
            pltpu.VMEM((rows, cols), jnp.int32),
            pltpu.VMEM((PEERS, bands, 2, LANES), bf16),
            pltpu.VMEM((PEERS, bands, 2, LANES), bf16),
            pltpu.VMEM((2, 1, cols), f32),
            pltpu.VMEM((2, 1, cols), f32),
            pltpu.VMEM((PEERS, 2, LANES), bf16),
            pltpu.VMEM((PEERS, 2, LANES), bf16),
            pltpu.VMEM((2, bands, PEERS, LANES), f32),
            pltpu.VMEM((2, PEERS, LANES), f32),
            pltpu.VMEM((CORE, X, Z, bands, 2, LANES), f32),
            pltpu.VMEM((2, 2 * bands, LANES), f32),
            pltpu.VMEM((Y, 1, LANES), f32),
            pltpu.VMEM((PEERS, 1, LANES), f32),
            dma, dma((Z,)), dma((2,)), dma((2,)), dma, dma,
            dma, dma, dma, dma((Z,)), dma((Z,)), dma, dma, dma, dma, dma,
            dma((2,)), pltpu.SemaphoreType.REGULAR((3,)),
        ],
        compiler_params=pltpu.CompilerParams(collective_id=0, has_side_effects=True, vmem_limit_bytes=8 << 20),
    )(pltpu.with_memory_space_constraint(stack[0], pltpu.HBM), pltpu.with_memory_space_constraint(cloud[0], pltpu.HBM))


def solution(mesh):
    placed = (P("date", None, "pix", None), P("date", "pix", None))
    return jax.shard_map(
        body, mesh=mesh, in_specs=placed, out_specs=P(None, "pix", None), check_vma=False
    )
```

```python
import functools

import jax
import jax.numpy as jnp
from jax import lax
from jax.experimental import pallas as pl
from jax.experimental.pallas import tpu as pltpu
from jax.sharding import PartitionSpec as P

ITERS = 2
DELTA_SQ = 0.01
EPS = 1e-05
MESH = pl.DeviceIdType.MESH
Z, X, CORE, Y = 8, 4, 2, 4
LINE = X * CORE
PEERS = Z * LINE
PAIRS = 4
ELDEST = 1
LANES = 128


def kernel(
    pixels, stack_hbm, cloud_hbm, out_ref,
    stack_ref, cloud_ref, send, recv, hsend, hrecv, vsend, vrecv, work, seen, gath, part, ymom, dmom, every, whole,
    s_stack, r_stack, s_halo, r_halo, s_valid, r_valid,
    s_z, s_x, s_core, r_z, r_x, r_core, s_ymom, r_ymom, s_dmom, r_dmom,
    s_in, far, s_every, r_every,
):
    bands = stack_ref.shape[0]
    rows, cols = cloud_ref.shape
    me = lax.axis_index("date")
    y = lax.axis_index("pix")
    z = me // (X * CORE)
    x = (me // CORE) % X
    core = me % CORE

    def date_at(zz, xx, cc):
        return (zz * X + xx) * CORE + cc

    def peer(step):
        return (me + step) % PEERS

    def in_line(zz, step):
        return zz * LINE + (me % LINE + step) % LINE

    def give(zz, first):
        @pl.loop(first, LINE)
        def _(step):
            to = in_line(zz, step)
            pltpu.make_async_remote_copy(
                src_ref=send.at[to], dst_ref=recv.at[me],
                send_sem=s_stack, recv_sem=r_stack.at[z],
                device_id={"date": to}, device_id_type=MESH,
            ).start()

    fetches = [
        pltpu.make_async_copy(cloud_hbm, cloud_ref, s_in.at[0]),
        pltpu.make_async_copy(stack_hbm, stack_ref, s_in.at[1]),
    ]

    barrier = pltpu.get_barrier_semaphore()
    for copy in fetches:
        copy.start()

    def greet(zz, first):
        @pl.loop(first, LINE)
        def _(step):
            pl.semaphore_signal(
                barrier, inc=1, device_id={"date": in_line(zz, step)}, device_id_type=MESH
            )

    for dz in (2, 6, 1, 7):
        greet((z + dz) % Z, 0)
    greet(z, 1)

    for step in range(1, Y):
        pl.semaphore_signal(barrier, inc=1, device_id={"pix": (y + step) % Y}, device_id_type=MESH)

    for copy in fetches:
        copy.wait()

    @pl.loop(0, Z)
    def _(zz):
        for cc in range(CORE):
            tile = pl.ds(pl.multiple_of((zz * CORE + cc) * LANES, LANES), LANES)
            for k in range(PAIRS):
                send[date_at(zz, k, cc)] = stack_ref[:, 2 * k : 2 * k + 2, tile]

    recv[me] = send[me]
    cloudy = (1 - cloud_ref[...]).astype(jnp.float32)
    hsend[0] = cloudy[0:1]
    hsend[1] = cloudy[rows - 1 : rows]

    pl.semaphore_wait(barrier, 5 * LINE - 1 + Y - 1)
    for slot, dz in enumerate((Z - 1, 1, Z - 2)):
        to = date_at((z + dz) % Z, x, core)
        pl.semaphore_signal(far.at[slot], inc=1, device_id={"date": to}, device_id_type=MESH)

    halos = []
    for side, to in ((0, (y + Y - 1) % Y), (1, (y + 1) % Y)):
        halos.append(
            pltpu.make_async_remote_copy(
                src_ref=hsend.at[side], dst_ref=hrecv.at[side],
                send_sem=s_halo.at[side], recv_sem=r_halo.at[side],
                device_id={"pix": to}, device_id_type=MESH,
            )
        )
    for copy in halos:
        copy.start()

    for dz in (2, 6, 1, 7):
        give((z + dz) % Z, 0)
    give(z, 1)
    for slot, dz in enumerate((3, 5, 4)):
        pl.semaphore_wait(far.at[slot], 1)
        give((z + dz) % Z, 0)

    for copy in halos:
        copy.wait()
    above = jnp.where(y > 0, hrecv[1], 0.0)
    below = jnp.where(y < Y - 1, hrecv[0], 0.0)
    row = lax.broadcasted_iota(jnp.int32, (rows, cols), 0)
    col = lax.broadcasted_iota(jnp.int32, (rows, cols), 1)
    near = jnp.maximum(cloudy, jnp.where(row == 0, above, pltpu.roll(cloudy, 1, 0)))
    near = jnp.maximum(near, jnp.where(row == rows - 1, below, pltpu.roll(cloudy, rows - 1, 0)))
    near = jnp.maximum(near, jnp.where(col == 0, 0.0, pltpu.roll(cloudy, 1, 1)))
    near = jnp.maximum(near, jnp.where(col == cols - 1, 0.0, pltpu.roll(cloudy, cols - 1, 1)))
    valid = 1.0 - near
    for c in range(Z * CORE):
        for k in range(PAIRS):
            block = valid[2 * k : 2 * k + 2, c * LANES : (c + 1) * LANES]
            vsend[date_at(c // CORE, k, c % CORE)] = block.astype(jnp.bfloat16)
    vrecv[me] = vsend[me]

    @pl.loop(1, PEERS)
    def _(step):
        to = peer(step)
        pltpu.make_async_remote_copy(
            src_ref=vsend.at[to], dst_ref=vrecv.at[me], send_sem=s_valid, recv_sem=r_valid,
            device_id={"date": to}, device_id_type=MESH,
        ).start()

    def taken(ref, count, sem):
        some = ref.at[pl.ds(0, count)]
        pltpu.make_async_copy(some, some, sem).wait()

    def unpack(zz):
        @pl.loop(0, LINE, unroll=True)
        def _(step):
            date = zz * LINE + step
            block = recv[date].astype(jnp.float32)
            for b in range(bands):
                for r in range(2):
                    work[r, b, pl.ds(date, 1), :] = block[b, r : r + 1]

    taken(recv, LINE - 1, r_stack.at[z])
    unpack(z)

    @pl.loop(1, Z)
    def _(step):
        zz = (z + step) % Z
        taken(recv, LINE, r_stack.at[zz])
        unpack(zz)

    taken(vrecv, PEERS - 1, r_valid)

    @pl.loop(0, PEERS, unroll=8)
    def _(date):
        block = vrecv[date].astype(jnp.float32)
        for r in range(2):
            seen[r, pl.ds(date, 1), :] = block[r : r + 1]

    medians = [[jnp.zeros((1, LANES), jnp.float32)] * bands for _ in range(2)]
    for step in range(ITERS + 1):
        for r in range(2):
            median = medians[r]
            numer = [jnp.zeros((8, LANES), jnp.float32)] * bands
            denom = jnp.zeros((8, LANES), jnp.float32)
            for j in range(0, PEERS, 8):
                values = [work[r, b, j : j + 8, :] for b in range(bands)]
                weight = seen[r, j : j + 8, :]
                if step > 0:
                    square = DELTA_SQ
                    for b in range(bands):
                        diff = values[b] - median[b]
                        square = square + diff * diff
                    weight = weight * lax.rsqrt(square)
                denom = denom + weight
                numer = [n + weight * v for n, v in zip(numer, values)]
            scale = 1.0 / (jnp.sum(denom, axis=0, keepdims=True) + 1.0)
            medians[r] = [
                (jnp.sum(n, axis=0, keepdims=True) + m) * scale for n, m in zip(numer, median)
            ]
    for r in range(2):
        for b in range(bands):
            median = medians[r][b]
            gath[core, x, z, b, r : r + 1, :] = median
            part[r, b : b + 1, :] = median
            part[r, bands + b : bands + b + 1, :] = median * median

    def pass_on(chunk, send_sem, recv_sem, to):
        pltpu.make_async_remote_copy(
            src_ref=gath.at[chunk], dst_ref=gath.at[chunk],
            send_sem=send_sem, recv_sem=recv_sem,
            device_id={"date": to}, device_id_type=MESH,
        ).start()

    for zz in (0, 1, 7, 2, 6, 3, 5, 4):

        @pl.when(zz != z)
        def _():
            pass_on((core, x, z), s_z, r_z.at[z], date_at(zz, x, core))

    def along_x(zz):
        for xx in (0, 1, 3, 2):

            @pl.when(xx != x)
            def _():
                pass_on((core, x, zz), s_x, r_x.at[zz], date_at(z, xx, core))

    along_x(z)
    pass_on((core, x, z), s_core, r_core, date_at(z, x, 1 - core))

    sums = jnp.sum(part[0] + part[1], axis=1, keepdims=True)
    lane = lax.broadcasted_iota(jnp.int32, (2 * bands, LANES), 1)
    which = lax.broadcasted_iota(jnp.int32, (2 * bands, LANES), 0)
    ymom[y] = jnp.sum(jnp.where(lane == which, sums, 0.0), axis=0, keepdims=True)
    for step in range(1, Y):
        pltpu.make_async_remote_copy(
            src_ref=ymom.at[y], dst_ref=ymom.at[y], send_sem=s_ymom, recv_sem=r_ymom,
            device_id={"pix": (y + step) % Y}, device_id_type=MESH,
        ).start()

    eldest = (me == ELDEST) & (y == 0)
    others = (me != ELDEST) | (y != 0)
    every[y * PEERS + me] = ymom[y]

    @pl.when(others)
    def _():
        pltpu.make_async_remote_copy(
            src_ref=every.at[y * PEERS + me], dst_ref=every.at[y * PEERS + me], send_sem=s_every, recv_sem=r_every,
            device_id={"date": ELDEST, "pix": 0}, device_id_type=MESH,
        ).start()
    def spread(step):
        zz = (z + step) % Z
        taken(gath.at[core, x], 1, r_z.at[zz])
        chunk = (core, x, zz)
        along_x(zz)
        pass_on(chunk, s_core, r_core, date_at(z, x, 1 - core))

    spread(1)
    spread(7)
    taken(ymom, Y - 1, r_ymom)
    dmom[me] = (ymom[0] + ymom[1]) + (ymom[2] + ymom[3])

    @pl.loop(0, PEERS)
    def _(to):
        @pl.when((to != me) & ((to != ELDEST) | (y != 0)))
        def _():
            pltpu.make_async_remote_copy(
                src_ref=dmom.at[me], dst_ref=dmom.at[me], send_sem=s_dmom, recv_sem=r_dmom,
                device_id={"date": to}, device_id_type=MESH,
            ).start()

    for step in (2, 6, 3, 5, 4):
        spread(step)
    for step in (0, 1, 7, 2, 6, 3, 5, 4):
        zz = (z + step) % Z
        taken(gath.at[core, x], X - 1, r_x.at[zz])
        for hop in (1, 3, 2):
            pass_on((core, (x + hop) % X, zz), s_core, r_core, date_at(z, x, 1 - core))

    @pl.when(others)
    def _():
        taken(dmom, PEERS - 1, r_dmom)
        total = dmom[0]
        for d in range(1, PEERS):
            total = total + dmom[d]
        whole[...] = total

    @pl.when(eldest)
    def _():
        taken(every, Y * PEERS - 1, r_every)

        def of_date(d):
            return (every[d] + every[PEERS + d]) + (every[2 * PEERS + d] + every[3 * PEERS + d])

        total = of_date(0)
        for d in range(1, PEERS):
            total = total + of_date(d)
        whole[...] = total

    total = whole[...]
    lane = lax.broadcasted_iota(jnp.int32, (1, LANES), 1)
    means, scales = [], []
    for b in range(bands):
        mean = jnp.sum(jnp.where(lane == b, total, 0.0), axis=1, keepdims=True) / pixels
        second = jnp.sum(jnp.where(lane == bands + b, total, 0.0), axis=1, keepdims=True) / pixels
        var = second - mean * mean
        means.append(mean)
        scales.append(1.0 / jnp.sqrt(var + EPS))

    pltpu.make_async_copy(gath.at[0], gath.at[0], r_core).wait()

    @pl.loop(0, Z)
    def _(zz):
        for cc in range(CORE):
            tile = pl.ds(pl.multiple_of((zz * CORE + cc) * LANES, LANES), LANES)
            for b in range(bands):
                block = jnp.concatenate([gath[cc, k, zz, b] for k in range(PAIRS)], axis=0)
                out_ref[b, :, tile] = (block - means[b]) * scales[b]

    taken(send, PEERS - 1, s_stack)
    taken(vsend, PEERS - 1, s_valid)
    @pl.when(others & (y == 0))
    def _():
        taken(dmom, PEERS - 2, s_dmom)

    @pl.when(eldest | (y != 0))
    def _():
        taken(dmom, PEERS - 1, s_dmom)

    @pl.when(others)
    def _():
        taken(every, 1, s_every)

    taken(ymom, Y - 1, s_ymom)
    taken(gath.at[0, 0], Z - 1, s_z)
    taken(gath.at[0], X - 1, s_x)
    pltpu.make_async_copy(gath.at[0], gath.at[0], s_core).wait()


def body(stack, cloud):
    _, bands, rows, cols = stack.shape
    pixels = float(lax.axis_size("pix") * rows * cols)
    f32, bf16 = jnp.float32, jnp.bfloat16
    dma = pltpu.SemaphoreType.DMA
    return pl.pallas_call(
        functools.partial(kernel, pixels),
        out_shape=jax.ShapeDtypeStruct((bands, rows, cols), f32),
        in_specs=[pl.BlockSpec(memory_space=pltpu.HBM)] * 2,
        out_specs=pl.BlockSpec(memory_space=pltpu.VMEM),
        scratch_shapes=[
            pltpu.VMEM((bands, rows, cols), bf16),
            pltpu.VMEM((rows, cols), jnp.int32),
            pltpu.VMEM((PEERS, bands, 2, LANES), bf16),
            pltpu.VMEM((PEERS, bands, 2, LANES), bf16),
            pltpu.VMEM((2, 1, cols), f32),
            pltpu.VMEM((2, 1, cols), f32),
            pltpu.VMEM((PEERS, 2, LANES), bf16),
            pltpu.VMEM((PEERS, 2, LANES), bf16),
            pltpu.VMEM((2, bands, PEERS, LANES), f32),
            pltpu.VMEM((2, PEERS, LANES), f32),
            pltpu.VMEM((CORE, X, Z, bands, 2, LANES), f32),
            pltpu.VMEM((2, 2 * bands, LANES), f32),
            pltpu.VMEM((Y, 1, LANES), f32),
            pltpu.VMEM((PEERS, 1, LANES), f32),
            pltpu.VMEM((Y * PEERS, 1, LANES), f32),
            pltpu.VMEM((1, LANES), f32),
            dma, dma((Z,)), dma((2,)), dma((2,)), dma, dma,
            dma, dma, dma, dma((Z,)), dma((Z,)), dma, dma, dma, dma, dma,
            dma((2,)), pltpu.SemaphoreType.REGULAR((3,)), dma, dma,
        ],
        compiler_params=pltpu.CompilerParams(collective_id=0, has_side_effects=True, vmem_limit_bytes=8 << 20),
    )(pltpu.with_memory_space_constraint(stack[0], pltpu.HBM), pltpu.with_memory_space_constraint(cloud[0], pltpu.HBM))


def solution(mesh):
    placed = (P("date", None, "pix", None), P("date", "pix", None))
    return jax.shard_map(
        body, mesh=mesh, in_specs=placed, out_specs=P(None, "pix", None), check_vma=False
    )
```

```python
import functools

import jax
import jax.numpy as jnp
from jax import lax
from jax.experimental import pallas as pl
from jax.experimental.pallas import tpu as pltpu
from jax.sharding import PartitionSpec as P

ITERS = 2
DELTA_SQ = 0.01
EPS = 1e-05
MESH = pl.DeviceIdType.MESH
Z, X, CORE, Y = 8, 4, 2, 4
LINE = X * CORE
PEERS = Z * LINE
PAIRS = 4
ELDEST = 1
LANES = 128


def kernel(
    pixels, stack_hbm, cloud_hbm, out_ref,
    stack_ref, cloud_ref, send, recv, hsend, hrecv, vsend, vrecv, work, seen, gath, part, ymom, dmom, every, whole,
    s_stack, r_stack, s_halo, r_halo, s_valid, r_valid,
    s_z, s_x, s_core, r_z, r_x, r_core, s_ymom, r_ymom, s_dmom, r_dmom,
    s_in, far, s_every, r_every, s_mid, s_late, s_far,
):
    bands = stack_ref.shape[0]
    rows, cols = cloud_ref.shape
    me = lax.axis_index("date")
    y = lax.axis_index("pix")
    z = me // (X * CORE)
    x = (me // CORE) % X
    core = me % CORE

    def date_at(zz, xx, cc):
        return (zz * X + xx) * CORE + cc

    def peer(step):
        return (me + step) % PEERS

    def in_line(zz, step):
        return zz * LINE + (me % LINE + step) % LINE

    def give(zz, first):
        @pl.loop(first, LINE)
        def _(step):
            to = in_line(zz, step)
            pltpu.make_async_remote_copy(
                src_ref=send.at[to], dst_ref=recv.at[me],
                send_sem=s_stack, recv_sem=r_stack.at[z],
                device_id={"date": to}, device_id_type=MESH,
            ).start()

    fetches = [
        pltpu.make_async_copy(cloud_hbm, cloud_ref, s_in.at[0]),
        pltpu.make_async_copy(stack_hbm, stack_ref, s_in.at[1]),
    ]

    barrier = pltpu.get_barrier_semaphore()
    for copy in fetches:
        copy.start()

    def greet(zz, first):
        @pl.loop(first, LINE)
        def _(step):
            pl.semaphore_signal(
                barrier, inc=1, device_id={"date": in_line(zz, step)}, device_id_type=MESH
            )

    for dz in (2, 6, 1, 7):
        greet((z + dz) % Z, 0)
    greet(z, 1)

    for step in range(1, Y):
        pl.semaphore_signal(barrier, inc=1, device_id={"pix": (y + step) % Y}, device_id_type=MESH)

    for copy in fetches:
        copy.wait()

    @pl.loop(0, Z)
    def _(zz):
        for cc in range(CORE):
            tile = pl.ds(pl.multiple_of((zz * CORE + cc) * LANES, LANES), LANES)
            for k in range(PAIRS):
                send[date_at(zz, k, cc)] = stack_ref[:, 2 * k : 2 * k + 2, tile]

    recv[me] = send[me]
    cloudy = (1 - cloud_ref[...]).astype(jnp.float32)
    hsend[0] = cloudy[0:1]
    hsend[1] = cloudy[rows - 1 : rows]

    pl.semaphore_wait(barrier, 5 * LINE - 1 + Y - 1)
    for slot, dz in enumerate((Z - 1, 1, Z - 2)):
        to = date_at((z + dz) % Z, x, core)
        pl.semaphore_signal(far.at[slot], inc=1, device_id={"date": to}, device_id_type=MESH)

    halos = []
    for side, to in ((0, (y + Y - 1) % Y), (1, (y + 1) % Y)):
        halos.append(
            pltpu.make_async_remote_copy(
                src_ref=hsend.at[side], dst_ref=hrecv.at[side],
                send_sem=s_halo.at[side], recv_sem=r_halo.at[side],
                device_id={"pix": to}, device_id_type=MESH,
            )
        )
    for copy in halos:
        copy.start()

    for dz in (2, 6):
        give((z + dz) % Z, 0)
    for slot, dz in enumerate((3, 5, 4)):
        pl.semaphore_wait(far.at[slot], 1)
        give((z + dz) % Z, 0)

    for copy in halos:
        copy.wait()
    above = jnp.where(y > 0, hrecv[1], 0.0)
    below = jnp.where(y < Y - 1, hrecv[0], 0.0)
    row = lax.broadcasted_iota(jnp.int32, (rows, cols), 0)
    col = lax.broadcasted_iota(jnp.int32, (rows, cols), 1)
    near = jnp.maximum(cloudy, jnp.where(row == 0, above, pltpu.roll(cloudy, 1, 0)))
    near = jnp.maximum(near, jnp.where(row == rows - 1, below, pltpu.roll(cloudy, rows - 1, 0)))
    near = jnp.maximum(near, jnp.where(col == 0, 0.0, pltpu.roll(cloudy, 1, 1)))
    near = jnp.maximum(near, jnp.where(col == cols - 1, 0.0, pltpu.roll(cloudy, cols - 1, 1)))
    valid = 1.0 - near
    for c in range(Z * CORE):
        for k in range(PAIRS):
            block = valid[2 * k : 2 * k + 2, c * LANES : (c + 1) * LANES]
            vsend[date_at(c // CORE, k, c % CORE)] = block.astype(jnp.bfloat16)
    vrecv[me] = vsend[me]

    @pl.loop(1, PEERS)
    def _(step):
        to = peer(step)
        pltpu.make_async_remote_copy(
            src_ref=vsend.at[to], dst_ref=vrecv.at[me], send_sem=s_valid, recv_sem=r_valid,
            device_id={"date": to}, device_id_type=MESH,
        ).start()

    for dz in (1, 7):
        give((z + dz) % Z, 0)
    give(z, 1)

    def taken(ref, count, sem):
        some = ref.at[pl.ds(0, count)]
        pltpu.make_async_copy(some, some, sem).wait()

    def rows_of(zz):
        return pl.ds(pl.multiple_of(2 * LINE * zz, 2 * LINE), 2 * LINE)

    def unpack(zz):
        for step in range(LINE):
            block = recv[zz * LINE + step].astype(jnp.float32)
            for b in range(bands):
                work.at[b, rows_of(zz)][2 * step : 2 * step + 2, :] = block[b]

    @pl.loop(2, Z - 1)
    def _(step):
        zz = (z + step) % Z
        taken(recv, LINE, r_stack.at[zz])
        unpack(zz)

    for step in (1, Z - 1):
        zz = (z + step) % Z
        taken(recv, LINE, r_stack.at[zz])
        unpack(zz)

    taken(recv, LINE - 1, r_stack.at[z])
    unpack(z)

    taken(vrecv, PEERS - 1, r_valid)

    @pl.loop(0, Z)
    def _(zz):
        for step in range(LINE):
            block = vrecv[zz * LINE + step].astype(jnp.float32)
            seen.at[rows_of(zz)][2 * step : 2 * step + 2, :] = block

    def over_dates(sums):
        sums = sums + pltpu.roll(sums, 2, 0)
        return sums + pltpu.roll(sums, 4, 0)

    median = [jnp.zeros((8, LANES), jnp.float32)] * bands
    for step in range(ITERS + 1):
        numer = [jnp.zeros((8, LANES), jnp.float32)] * bands
        denom = jnp.zeros((8, LANES), jnp.float32)
        for j in range(0, 2 * PEERS, 8):
            values = [work[b, j : j + 8, :] for b in range(bands)]
            weight = seen[j : j + 8, :]
            if step > 0:
                square = DELTA_SQ
                for b in range(bands):
                    diff = values[b] - median[b]
                    square = square + diff * diff
                weight = weight * lax.rsqrt(square)
            denom = denom + weight
            numer = [n + weight * v for n, v in zip(numer, values)]
        scale = 1.0 / (over_dates(denom) + 1.0)
        median = [(over_dates(n) + m) * scale for n, m in zip(numer, median)]
    for b in range(bands):
        gath[core, x, z, b] = median[b][0:2]
        square = median[b] * median[b]
        part[b : b + 1, :] = median[b][0:1] + median[b][1:2]
        part[bands + b : bands + b + 1, :] = square[0:1] + square[1:2]

    def pass_on(chunk, send_sem, recv_sem, to):
        pltpu.make_async_remote_copy(
            src_ref=gath.at[chunk], dst_ref=gath.at[chunk],
            send_sem=send_sem, recv_sem=recv_sem,
            device_id={"date": to}, device_id_type=MESH,
        ).start()

    for zz in (0, 1, 7, 2, 6, 3, 5, 4):

        @pl.when(zz != z)
        def _():
            pass_on((core, x, z), s_z, r_z.at[z], date_at(zz, x, core))

    def along_x(zz):
        for xx in (0, 1, 3, 2):

            @pl.when(xx != x)
            def _():
                pass_on((core, x, zz), s_x, r_x.at[zz], date_at(z, xx, core))

    distant = (z >= 3) & (z <= 5) & (x != 0) & (core == 0)

    @pl.when(distant)
    def _():
        pass_on((core, x, z), s_far, r_core, ELDEST)

    along_x(z)
    pass_on((core, x, z), s_core, r_core, date_at(z, x, 1 - core))

    sums = jnp.sum(part[...], axis=1, keepdims=True)
    lane = lax.broadcasted_iota(jnp.int32, (2 * bands, LANES), 1)
    which = lax.broadcasted_iota(jnp.int32, (2 * bands, LANES), 0)
    ymom[y] = jnp.sum(jnp.where(lane == which, sums, 0.0), axis=0, keepdims=True)
    for step in range(1, Y):
        pltpu.make_async_remote_copy(
            src_ref=ymom.at[y], dst_ref=ymom.at[y], send_sem=s_ymom, recv_sem=r_ymom,
            device_id={"pix": (y + step) % Y}, device_id_type=MESH,
        ).start()

    eldest = (me == ELDEST) & (y == 0)
    others = (me != ELDEST) | (y != 0)
    every[y * PEERS + me] = ymom[y]

    @pl.when(others)
    def _():
        pltpu.make_async_remote_copy(
            src_ref=every.at[y * PEERS + me], dst_ref=every.at[y * PEERS + me], send_sem=s_every, recv_sem=r_every,
            device_id={"date": ELDEST, "pix": 0}, device_id_type=MESH,
        ).start()
    def spread(step):
        zz = (z + step) % Z
        taken(gath.at[core, x], 1, r_z.at[zz])
        chunk = (core, x, zz)
        along_x(zz)
        pass_on(chunk, s_core, r_core, date_at(z, x, 1 - core))

    spread(1)
    spread(7)
    taken(ymom, Y - 1, r_ymom)
    dmom[me] = (ymom[0] + ymom[1]) + (ymom[2] + ymom[3])

    @pl.loop(0, PEERS)
    def _(to):
        @pl.when((to != me) & ((to != ELDEST) | (y != 0)))
        def _():
            pltpu.make_async_remote_copy(
                src_ref=dmom.at[me], dst_ref=dmom.at[me], send_sem=s_dmom, recv_sem=r_dmom,
                device_id={"date": to}, device_id_type=MESH,
            ).start()

    for step in (2, 6, 3, 5, 4):
        spread(step)
    elsewhere = (z != 0) | (x != 0) | (core != 0)
    for step in (0, 1, 7, 2, 6, 3, 5, 4):
        zz = (z + step) % Z
        taken(gath.at[core, x], X - 1, r_x.at[zz])

        def hand_over(send_sem):
            for hop in (1, 3, 2):
                pass_on((core, (x + hop) % X, zz), send_sem, r_core, date_at(z, x, 1 - core))

        if step in (3, 5, 4):

            @pl.when(elsewhere)
            def _():
                hand_over(s_late)

        else:
            hand_over(s_mid)

    @pl.when(others)
    def _():
        taken(dmom, PEERS - 1, r_dmom)
        total = dmom[0]
        for d in range(1, PEERS):
            total = total + dmom[d]
        whole[...] = total

    @pl.when(eldest)
    def _():
        taken(every, Y * PEERS - 1, r_every)

        def of_date(d):
            return (every[d] + every[PEERS + d]) + (every[2 * PEERS + d] + every[3 * PEERS + d])

        total = of_date(0)
        for d in range(1, PEERS):
            total = total + of_date(d)
        whole[...] = total

    total = whole[...]
    lane = lax.broadcasted_iota(jnp.int32, (1, LANES), 1)
    means, scales = [], []
    for b in range(bands):
        mean = jnp.sum(jnp.where(lane == b, total, 0.0), axis=1, keepdims=True) / pixels
        second = jnp.sum(jnp.where(lane == bands + b, total, 0.0), axis=1, keepdims=True) / pixels
        var = second - mean * mean
        means.append(mean)
        scales.append(1.0 / jnp.sqrt(var + EPS))

    pltpu.make_async_copy(gath.at[0], gath.at[0], r_core).wait()

    @pl.loop(0, Z)
    def _(zz):
        for cc in range(CORE):
            tile = pl.ds(pl.multiple_of((zz * CORE + cc) * LANES, LANES), LANES)
            for b in range(bands):
                block = jnp.concatenate([gath[cc, k, zz, b] for k in range(PAIRS)], axis=0)
                out_ref[b, :, tile] = (block - means[b]) * scales[b]

    taken(send, PEERS - 1, s_stack)
    taken(vsend, PEERS - 1, s_valid)
    @pl.when(others & (y == 0))
    def _():
        taken(dmom, PEERS - 2, s_dmom)

    @pl.when(eldest | (y != 0))
    def _():
        taken(dmom, PEERS - 1, s_dmom)

    @pl.when(others)
    def _():
        taken(every, 1, s_every)

    taken(ymom, Y - 1, s_ymom)
    taken(gath.at[0, 0], Z - 1, s_z)
    taken(gath.at[0], X - 1, s_x)
    taken(gath.at[0], 1, s_core)
    mid = gath.at[0, pl.ds(0, X - 1), pl.ds(0, Z - 3)]
    pltpu.make_async_copy(mid, mid, s_mid).wait()

    @pl.when(elsewhere)
    def _():
        late = gath.at[0, pl.ds(0, X - 1), pl.ds(0, 3)]
        pltpu.make_async_copy(late, late, s_late).wait()

    @pl.when(distant)
    def _():
        taken(gath.at[0, 0], 1, s_far)


def body(stack, cloud):
    _, bands, rows, cols = stack.shape
    pixels = float(lax.axis_size("pix") * rows * cols)
    f32, bf16 = jnp.float32, jnp.bfloat16
    dma = pltpu.SemaphoreType.DMA
    return pl.pallas_call(
        functools.partial(kernel, pixels),
        out_shape=jax.ShapeDtypeStruct((bands, rows, cols), f32),
        in_specs=[pl.BlockSpec(memory_space=pltpu.HBM)] * 2,
        out_specs=pl.BlockSpec(memory_space=pltpu.VMEM),
        scratch_shapes=[
            pltpu.VMEM((bands, rows, cols), bf16),
            pltpu.VMEM((rows, cols), jnp.int32),
            pltpu.VMEM((PEERS, bands, 2, LANES), bf16),
            pltpu.VMEM((PEERS, bands, 2, LANES), bf16),
            pltpu.VMEM((2, 1, cols), f32),
            pltpu.VMEM((2, 1, cols), f32),
            pltpu.VMEM((PEERS, 2, LANES), bf16),
            pltpu.VMEM((PEERS, 2, LANES), bf16),
            pltpu.VMEM((bands, 2 * PEERS, LANES), f32),
            pltpu.VMEM((2 * PEERS, LANES), f32),
            pltpu.VMEM((CORE, X, Z, bands, 2, LANES), f32),
            pltpu.VMEM((2 * bands, LANES), f32),
            pltpu.VMEM((Y, 1, LANES), f32),
            pltpu.VMEM((PEERS, 1, LANES), f32),
            pltpu.VMEM((Y * PEERS, 1, LANES), f32),
            pltpu.VMEM((1, LANES), f32),
            dma, dma((Z,)), dma((2,)), dma((2,)), dma, dma,
            dma, dma, dma, dma((Z,)), dma((Z,)), dma, dma, dma, dma, dma,
            dma((2,)), pltpu.SemaphoreType.REGULAR((3,)), dma, dma, dma, dma, dma,
        ],
        compiler_params=pltpu.CompilerParams(collective_id=0, has_side_effects=True, vmem_limit_bytes=8 << 20),
    )(pltpu.with_memory_space_constraint(stack[0], pltpu.HBM), pltpu.with_memory_space_constraint(cloud[0], pltpu.HBM))


def solution(mesh):
    placed = (P("date", None, "pix", None), P("date", "pix", None))
    return jax.shard_map(
        body, mesh=mesh, in_specs=placed, out_specs=P(None, "pix", None), check_vma=False
    )
```

```python
import functools

import jax
import jax.numpy as jnp
from jax import lax
from jax.experimental import pallas as pl
from jax.experimental.pallas import tpu as pltpu
from jax.sharding import PartitionSpec as P

ITERS = 2
DELTA_SQ = 0.01
EPS = 1e-05
MESH = pl.DeviceIdType.MESH
Z, X, CORE, Y = 8, 4, 2, 4
LINE = X * CORE
PEERS = Z * LINE
PAIRS = 4
ELDEST = 1
LANES = 128


def kernel(
    pixels, stack_hbm, cloud_hbm, out_ref,
    stack_ref, cloud_ref, send, recv, hsend, hrecv, vsend, vrecv, work, seen, gath, part, ymom, dmom, every, whole,
    s_stack, r_stack, s_halo, r_halo, s_valid, r_valid,
    s_z, s_x, s_core, r_z, r_x, r_core, s_ymom, r_ymom, s_dmom, r_dmom,
    s_in, far, s_every, r_every, s_mid, s_late, s_far,
):
    bands = stack_ref.shape[0]
    rows, cols = cloud_ref.shape
    me = lax.axis_index("date")
    y = lax.axis_index("pix")
    z = me // (X * CORE)
    x = (me // CORE) % X
    core = me % CORE

    def date_at(zz, xx, cc):
        return (zz * X + xx) * CORE + cc

    def peer(step):
        return (me + step) % PEERS

    def in_line(zz, step):
        return zz * LINE + (me % LINE + step) % LINE

    def give(zz, first):
        @pl.loop(first, LINE)
        def _(step):
            to = in_line(zz, step)
            pltpu.make_async_remote_copy(
                src_ref=send.at[to], dst_ref=recv.at[me],
                send_sem=s_stack, recv_sem=r_stack.at[z],
                device_id={"date": to}, device_id_type=MESH,
            ).start()

    fetches = [
        pltpu.make_async_copy(cloud_hbm, cloud_ref, s_in.at[0]),
        pltpu.make_async_copy(stack_hbm, stack_ref, s_in.at[1]),
    ]

    barrier = pltpu.get_barrier_semaphore()
    for copy in fetches:
        copy.start()

    def greet(zz, first):
        @pl.loop(first, LINE)
        def _(step):
            pl.semaphore_signal(
                barrier, inc=1, device_id={"date": in_line(zz, step)}, device_id_type=MESH
            )

    for dz in (2, 6, 1, 7):
        greet((z + dz) % Z, 0)
    greet(z, 1)

    for step in range(1, Y):
        pl.semaphore_signal(barrier, inc=1, device_id={"pix": (y + step) % Y}, device_id_type=MESH)

    for copy in fetches:
        copy.wait()

    @pl.loop(0, Z)
    def _(zz):
        for cc in range(CORE):
            tile = pl.ds(pl.multiple_of((zz * CORE + cc) * LANES, LANES), LANES)
            for k in range(PAIRS):
                send[date_at(zz, k, cc)] = stack_ref[:, 2 * k : 2 * k + 2, tile]

    recv[me] = send[me]
    cloudy = (1 - cloud_ref[...]).astype(jnp.float32)
    hsend[0] = cloudy[0:1]
    hsend[1] = cloudy[rows - 1 : rows]

    pl.semaphore_wait(barrier, 5 * LINE - 1 + Y - 1)
    for slot, dz in enumerate((Z - 1, 1, Z - 2)):
        to = date_at((z + dz) % Z, x, core)
        pl.semaphore_signal(far.at[slot], inc=1, device_id={"date": to}, device_id_type=MESH)

    halos = []
    for side, to in ((0, (y + Y - 1) % Y), (1, (y + 1) % Y)):
        halos.append(
            pltpu.make_async_remote_copy(
                src_ref=hsend.at[side], dst_ref=hrecv.at[side],
                send_sem=s_halo.at[side], recv_sem=r_halo.at[side],
                device_id={"pix": to}, device_id_type=MESH,
            )
        )
    for copy in halos:
        copy.start()

    for dz in (2, 6):
        give((z + dz) % Z, 0)
    for slot, dz in enumerate((3, 5, 4)):
        pl.semaphore_wait(far.at[slot], 1)
        give((z + dz) % Z, 0)

    for copy in halos:
        copy.wait()
    above = jnp.where(y > 0, hrecv[1], 0.0)
    below = jnp.where(y < Y - 1, hrecv[0], 0.0)
    row = lax.broadcasted_iota(jnp.int32, (rows, cols), 0)
    col = lax.broadcasted_iota(jnp.int32, (rows, cols), 1)
    near = jnp.maximum(cloudy, jnp.where(row == 0, above, pltpu.roll(cloudy, 1, 0)))
    near = jnp.maximum(near, jnp.where(row == rows - 1, below, pltpu.roll(cloudy, rows - 1, 0)))
    near = jnp.maximum(near, jnp.where(col == 0, 0.0, pltpu.roll(cloudy, 1, 1)))
    near = jnp.maximum(near, jnp.where(col == cols - 1, 0.0, pltpu.roll(cloudy, cols - 1, 1)))
    valid = 1.0 - near
    for c in range(Z * CORE):
        for k in range(PAIRS):
            block = valid[2 * k : 2 * k + 2, c * LANES : (c + 1) * LANES]
            vsend[date_at(c // CORE, k, c % CORE)] = block.astype(jnp.bfloat16)
    vrecv[me] = vsend[me]

    @pl.loop(1, PEERS)
    def _(step):
        to = peer(step)
        pltpu.make_async_remote_copy(
            src_ref=vsend.at[to], dst_ref=vrecv.at[me], send_sem=s_valid, recv_sem=r_valid,
            device_id={"date": to}, device_id_type=MESH,
        ).start()

    for dz in (1, 7):
        give((z + dz) % Z, 0)
    give(z, 1)

    def taken(ref, count, sem):
        some = ref.at[pl.ds(0, count)]
        pltpu.make_async_copy(some, some, sem).wait()

    def rows_of(zz):
        return pl.ds(pl.multiple_of(2 * LINE * zz, 2 * LINE), 2 * LINE)

    def unpack(zz):
        for step in range(LINE):
            block = recv[zz * LINE + step].astype(jnp.float32)
            for b in range(bands):
                work.at[b, rows_of(zz)][2 * step : 2 * step + 2, :] = block[b]

    @pl.loop(2, Z - 1)
    def _(step):
        zz = (z + step) % Z
        taken(recv, LINE, r_stack.at[zz])
        unpack(zz)

    for step in (1, Z - 1):
        zz = (z + step) % Z
        taken(recv, LINE, r_stack.at[zz])
        unpack(zz)

    taken(recv, LINE - 1, r_stack.at[z])
    unpack(z)

    taken(vrecv, PEERS - 1, r_valid)

    @pl.loop(0, Z)
    def _(zz):
        for step in range(LINE):
            block = vrecv[zz * LINE + step].astype(jnp.float32)
            seen.at[rows_of(zz)][2 * step : 2 * step + 2, :] = block

    def over_dates(sums):
        sums = sums + pltpu.roll(sums, 2, 0)
        return sums + pltpu.roll(sums, 4, 0)

    median = [jnp.zeros((8, LANES), jnp.float32)] * bands
    for step in range(ITERS + 1):
        numer = [jnp.zeros((8, LANES), jnp.float32)] * bands
        denom = jnp.zeros((8, LANES), jnp.float32)
        for j in range(0, 2 * PEERS, 8):
            values = [work[b, j : j + 8, :] for b in range(bands)]
            weight = seen[j : j + 8, :]
            if step > 0:
                square = DELTA_SQ
                for b in range(bands):
                    diff = values[b] - median[b]
                    square = square + diff * diff
                weight = weight * lax.rsqrt(square)
            denom = denom + weight
            numer = [n + weight * v for n, v in zip(numer, values)]
        scale = 1.0 / (over_dates(denom) + 1.0)
        median = [(over_dates(n) + m) * scale for n, m in zip(numer, median)]
    for b in range(bands):
        gath[core, x, z, b] = median[b][0:2]
        square = median[b] * median[b]
        part[b : b + 1, :] = median[b][0:1] + median[b][1:2]
        part[bands + b : bands + b + 1, :] = square[0:1] + square[1:2]

    def pass_on(chunk, send_sem, recv_sem, to):
        pltpu.make_async_remote_copy(
            src_ref=gath.at[chunk], dst_ref=gath.at[chunk],
            send_sem=send_sem, recv_sem=recv_sem,
            device_id={"date": to}, device_id_type=MESH,
        ).start()

    for zz in (0, 1, 7, 2, 6, 3, 5, 4):

        @pl.when(zz != z)
        def _():
            pass_on((core, x, z), s_z, r_z.at[z], date_at(zz, x, core))

    def along_x(zz):
        for xx in (0, 1, 3, 2):

            @pl.when(xx != x)
            def _():
                pass_on((core, x, zz), s_x, r_x.at[zz], date_at(z, xx, core))

    distant = (z >= 3) & (z <= 5) & (x != 0) & (core == 0)

    @pl.when(distant)
    def _():
        pass_on((core, x, z), s_far, r_core, ELDEST)

    along_x(z)
    pass_on((core, x, z), s_core, r_core, date_at(z, x, 1 - core))

    sums = jnp.sum(part[...], axis=1, keepdims=True)
    lane = lax.broadcasted_iota(jnp.int32, (2 * bands, LANES), 1)
    which = lax.broadcasted_iota(jnp.int32, (2 * bands, LANES), 0)
    ymom[y] = jnp.sum(jnp.where(lane == which, sums, 0.0), axis=0, keepdims=True)
    for step in range(1, Y):
        pltpu.make_async_remote_copy(
            src_ref=ymom.at[y], dst_ref=ymom.at[y], send_sem=s_ymom, recv_sem=r_ymom,
            device_id={"pix": (y + step) % Y}, device_id_type=MESH,
        ).start()

    eldest = (me == ELDEST) & (y == 0)
    others = (me != ELDEST) | (y != 0)
    every[y * PEERS + me] = ymom[y]

    @pl.when(others)
    def _():
        pltpu.make_async_remote_copy(
            src_ref=every.at[y * PEERS + me], dst_ref=every.at[y * PEERS + me], send_sem=s_every, recv_sem=r_every,
            device_id={"date": ELDEST, "pix": 0}, device_id_type=MESH,
        ).start()
    def spread(step):
        zz = (z + step) % Z
        taken(gath.at[core, x], 1, r_z.at[zz])
        chunk = (core, x, zz)
        along_x(zz)
        pass_on(chunk, s_core, r_core, date_at(z, x, 1 - core))

    spread(1)
    spread(7)
    taken(ymom, Y - 1, r_ymom)
    dmom[me] = (ymom[0] + ymom[1]) + (ymom[2] + ymom[3])

    @pl.loop(0, PEERS)
    def _(to):
        @pl.when((to != me) & ((to != ELDEST) | (y != 0)))
        def _():
            pltpu.make_async_remote_copy(
                src_ref=dmom.at[me], dst_ref=dmom.at[me], send_sem=s_dmom, recv_sem=r_dmom,
                device_id={"date": to}, device_id_type=MESH,
            ).start()

    for step in (2, 6, 3, 5, 4):
        spread(step)
    elsewhere = (z != 0) | (x != 0) | (core != 0)
    for step in (0, 1, 7, 2, 6, 3, 5, 4):
        zz = (z + step) % Z
        taken(gath.at[core, x], X - 1, r_x.at[zz])

        def hand_over(send_sem):
            for hop in (1, 3, 2):
                pass_on((core, (x + hop) % X, zz), send_sem, r_core, date_at(z, x, 1 - core))

        if step in (3, 5, 4):

            @pl.when(elsewhere)
            def _():
                hand_over(s_late)

        else:
            hand_over(s_mid)

    @pl.when(others)
    def _():
        taken(dmom, PEERS - 1, r_dmom)
        total = dmom[0]
        for d in range(1, PEERS):
            total = total + dmom[d]
        whole[...] = total

    @pl.when(eldest)
    def _():
        taken(every, Y * PEERS - 1, r_every)

        def of_date(d):
            return (every[d] + every[PEERS + d]) + (every[2 * PEERS + d] + every[3 * PEERS + d])

        total = of_date(0)
        for d in range(1, PEERS):
            total = total + of_date(d)
        whole[...] = total

    total = whole[...]
    lane = lax.broadcasted_iota(jnp.int32, (1, LANES), 1)
    means, scales = [], []
    for b in range(bands):
        mean = jnp.sum(jnp.where(lane == b, total, 0.0), axis=1, keepdims=True) / pixels
        second = jnp.sum(jnp.where(lane == bands + b, total, 0.0), axis=1, keepdims=True) / pixels
        var = second - mean * mean
        means.append(mean)
        scales.append(1.0 / jnp.sqrt(var + EPS))

    def settle(cc):
        @pl.loop(0, Z)
        def _(zz):
            tile = pl.ds(pl.multiple_of((zz * CORE + cc) * LANES, LANES), LANES)
            for b in range(bands):
                block = jnp.concatenate([gath[cc, k, zz, b] for k in range(PAIRS)], axis=0)
                out_ref[b, :, tile] = (block - means[b]) * scales[b]

    settle(core)
    pltpu.make_async_copy(gath.at[0], gath.at[0], r_core).wait()
    settle(1 - core)

    taken(send, PEERS - 1, s_stack)
    taken(vsend, PEERS - 1, s_valid)
    @pl.when(others & (y == 0))
    def _():
        taken(dmom, PEERS - 2, s_dmom)

    @pl.when(eldest | (y != 0))
    def _():
        taken(dmom, PEERS - 1, s_dmom)

    @pl.when(others)
    def _():
        taken(every, 1, s_every)

    taken(ymom, Y - 1, s_ymom)
    taken(gath.at[0, 0], Z - 1, s_z)
    taken(gath.at[0], X - 1, s_x)
    taken(gath.at[0], 1, s_core)
    mid = gath.at[0, pl.ds(0, X - 1), pl.ds(0, Z - 3)]
    pltpu.make_async_copy(mid, mid, s_mid).wait()

    @pl.when(elsewhere)
    def _():
        late = gath.at[0, pl.ds(0, X - 1), pl.ds(0, 3)]
        pltpu.make_async_copy(late, late, s_late).wait()

    @pl.when(distant)
    def _():
        taken(gath.at[0, 0], 1, s_far)


def body(stack, cloud):
    _, bands, rows, cols = stack.shape
    pixels = float(lax.axis_size("pix") * rows * cols)
    f32, bf16 = jnp.float32, jnp.bfloat16
    dma = pltpu.SemaphoreType.DMA
    return pl.pallas_call(
        functools.partial(kernel, pixels),
        out_shape=jax.ShapeDtypeStruct((bands, rows, cols), f32),
        in_specs=[pl.BlockSpec(memory_space=pltpu.HBM)] * 2,
        out_specs=pl.BlockSpec(memory_space=pltpu.VMEM),
        scratch_shapes=[
            pltpu.VMEM((bands, rows, cols), bf16),
            pltpu.VMEM((rows, cols), jnp.int32),
            pltpu.VMEM((PEERS, bands, 2, LANES), bf16),
            pltpu.VMEM((PEERS, bands, 2, LANES), bf16),
            pltpu.VMEM((2, 1, cols), f32),
            pltpu.VMEM((2, 1, cols), f32),
            pltpu.VMEM((PEERS, 2, LANES), bf16),
            pltpu.VMEM((PEERS, 2, LANES), bf16),
            pltpu.VMEM((bands, 2 * PEERS, LANES), f32),
            pltpu.VMEM((2 * PEERS, LANES), f32),
            pltpu.VMEM((CORE, X, Z, bands, 2, LANES), f32),
            pltpu.VMEM((2 * bands, LANES), f32),
            pltpu.VMEM((Y, 1, LANES), f32),
            pltpu.VMEM((PEERS, 1, LANES), f32),
            pltpu.VMEM((Y * PEERS, 1, LANES), f32),
            pltpu.VMEM((1, LANES), f32),
            dma, dma((Z,)), dma((2,)), dma((2,)), dma, dma,
            dma, dma, dma, dma((Z,)), dma((Z,)), dma, dma, dma, dma, dma,
            dma((2,)), pltpu.SemaphoreType.REGULAR((3,)), dma, dma, dma, dma, dma,
        ],
        compiler_params=pltpu.CompilerParams(collective_id=0, has_side_effects=True, vmem_limit_bytes=8 << 20),
    )(pltpu.with_memory_space_constraint(stack[0], pltpu.HBM), pltpu.with_memory_space_constraint(cloud[0], pltpu.HBM))


def solution(mesh):
    placed = (P("date", None, "pix", None), P("date", "pix", None))
    return jax.shard_map(
        body, mesh=mesh, in_specs=placed, out_specs=P(None, "pix", None), check_vma=False
    )
```

```python
import functools

import jax
import jax.numpy as jnp
from jax import lax
from jax.experimental import pallas as pl
from jax.experimental.pallas import tpu as pltpu
from jax.sharding import PartitionSpec as P

ITERS = 2
DELTA_SQ = 0.01
EPS = 1e-05
MESH = pl.DeviceIdType.MESH
Z, X, CORE, Y = 8, 4, 2, 4
LINE = X * CORE
PEERS = Z * LINE
PAIRS = 4
ELDEST = 1
LANES = 128


def kernel(
    pixels, stack_hbm, cloud_hbm, out_ref,
    stack_ref, cloud_ref, send, recv, hsend, hrecv, vsend, vrecv, work, seen, gath, part, ymom, dmom, every, whole,
    s_stack, r_stack, s_halo, r_halo, s_valid, r_valid,
    s_z, s_x, s_core, r_z, r_x, r_core, s_ymom, r_ymom, s_dmom, r_dmom,
    s_in, far, s_every, r_every, s_mid, s_late, s_far,
):
    bands = stack_ref.shape[0]
    rows, cols = cloud_ref.shape
    me = lax.axis_index("date")
    y = lax.axis_index("pix")
    z = me // (X * CORE)
    x = (me // CORE) % X
    core = me % CORE

    def date_at(zz, xx, cc):
        return (zz * X + xx) * CORE + cc

    def peer(step):
        return (me + step) % PEERS

    def in_line(zz, step):
        return zz * LINE + (me % LINE + step) % LINE

    def give(zz, first):
        @pl.loop(first, LINE)
        def _(step):
            to = in_line(zz, step)
            pltpu.make_async_remote_copy(
                src_ref=send.at[to], dst_ref=recv.at[me],
                send_sem=s_stack, recv_sem=r_stack.at[z],
                device_id={"date": to}, device_id_type=MESH,
            ).start()

    fetches = [
        pltpu.make_async_copy(cloud_hbm, cloud_ref, s_in.at[0]),
        pltpu.make_async_copy(stack_hbm, stack_ref, s_in.at[1]),
    ]

    barrier = pltpu.get_barrier_semaphore()
    for copy in fetches:
        copy.start()

    def greet(zz, first):
        @pl.loop(first, LINE)
        def _(step):
            pl.semaphore_signal(
                barrier, inc=1, device_id={"date": in_line(zz, step)}, device_id_type=MESH
            )

    for dz in (2, 6, 1, 7):
        greet((z + dz) % Z, 0)
    greet(z, 1)

    for step in range(1, Y):
        pl.semaphore_signal(barrier, inc=1, device_id={"pix": (y + step) % Y}, device_id_type=MESH)

    for copy in fetches:
        copy.wait()

    @pl.loop(0, Z)
    def _(zz):
        for cc in range(CORE):
            tile = pl.ds(pl.multiple_of((zz * CORE + cc) * LANES, LANES), LANES)
            for k in range(PAIRS):
                send[date_at(zz, k, cc)] = stack_ref[:, 2 * k : 2 * k + 2, tile]

    recv[me] = send[me]
    cloudy = (1 - cloud_ref[...]).astype(jnp.float32)
    hsend[0] = cloudy[0:1]
    hsend[1] = cloudy[rows - 1 : rows]

    pl.semaphore_wait(barrier, 5 * LINE - 1 + Y - 1)
    for slot, dz in enumerate((Z - 1, 1, Z - 2)):
        to = date_at((z + dz) % Z, x, core)
        pl.semaphore_signal(far.at[slot], inc=1, device_id={"date": to}, device_id_type=MESH)

    halos = []
    for side, to in ((0, (y + Y - 1) % Y), (1, (y + 1) % Y)):
        halos.append(
            pltpu.make_async_remote_copy(
                src_ref=hsend.at[side], dst_ref=hrecv.at[side],
                send_sem=s_halo.at[side], recv_sem=r_halo.at[side],
                device_id={"pix": to}, device_id_type=MESH,
            )
        )
    for copy in halos:
        copy.start()

    for dz in (2, 6):
        give((z + dz) % Z, 0)
    for slot, dz in enumerate((3, 5, 4)):
        pl.semaphore_wait(far.at[slot], 1)
        give((z + dz) % Z, 0)

    for copy in halos:
        copy.wait()
    above = jnp.where(y > 0, hrecv[1], 0.0)
    below = jnp.where(y < Y - 1, hrecv[0], 0.0)
    row = lax.broadcasted_iota(jnp.int32, (rows, cols), 0)
    col = lax.broadcasted_iota(jnp.int32, (rows, cols), 1)
    near = jnp.maximum(cloudy, jnp.where(row == 0, above, pltpu.roll(cloudy, 1, 0)))
    near = jnp.maximum(near, jnp.where(row == rows - 1, below, pltpu.roll(cloudy, rows - 1, 0)))
    near = jnp.maximum(near, jnp.where(col == 0, 0.0, pltpu.roll(cloudy, 1, 1)))
    near = jnp.maximum(near, jnp.where(col == cols - 1, 0.0, pltpu.roll(cloudy, cols - 1, 1)))
    valid = 1.0 - near
    for c in range(Z * CORE):
        for k in range(PAIRS):
            block = valid[2 * k : 2 * k + 2, c * LANES : (c + 1) * LANES]
            vsend[date_at(c // CORE, k, c % CORE)] = block.astype(jnp.bfloat16)
    vrecv[me] = vsend[me]

    @pl.loop(1, PEERS)
    def _(step):
        to = peer(step)
        pltpu.make_async_remote_copy(
            src_ref=vsend.at[to], dst_ref=vrecv.at[me], send_sem=s_valid, recv_sem=r_valid,
            device_id={"date": to}, device_id_type=MESH,
        ).start()

    for dz in (1, 7):
        give((z + dz) % Z, 0)
    give(z, 1)

    def taken(ref, count, sem):
        some = ref.at[pl.ds(0, count)]
        pltpu.make_async_copy(some, some, sem).wait()

    def rows_of(zz):
        return pl.ds(pl.multiple_of(2 * LINE * zz, 2 * LINE), 2 * LINE)

    def unpack(zz):
        for step in range(LINE):
            block = recv[zz * LINE + step].astype(jnp.float32)
            for b in range(bands):
                work.at[b, rows_of(zz)][2 * step : 2 * step + 2, :] = block[b]

    @pl.loop(2, Z - 1)
    def _(step):
        zz = (z + step) % Z
        taken(recv, LINE, r_stack.at[zz])
        unpack(zz)

    for step in (1, Z - 1):
        zz = (z + step) % Z
        taken(recv, LINE, r_stack.at[zz])
        unpack(zz)

    taken(recv, LINE - 1, r_stack.at[z])
    unpack(z)

    taken(vrecv, PEERS - 1, r_valid)

    @pl.loop(0, Z)
    def _(zz):
        for step in range(LINE):
            block = vrecv[zz * LINE + step].astype(jnp.float32)
            seen.at[rows_of(zz)][2 * step : 2 * step + 2, :] = block

    def over_dates(sums):
        sums = sums + pltpu.roll(sums, 2, 0)
        return sums + pltpu.roll(sums, 4, 0)

    median = [jnp.zeros((8, LANES), jnp.float32)] * bands
    for step in range(ITERS + 1):
        numer = [jnp.zeros((8, LANES), jnp.float32)] * bands
        denom = jnp.zeros((8, LANES), jnp.float32)
        for j in range(0, 2 * PEERS, 8):
            values = [work[b, j : j + 8, :] for b in range(bands)]
            weight = seen[j : j + 8, :]
            if step > 0:
                square = DELTA_SQ
                for b in range(bands):
                    diff = values[b] - median[b]
                    square = square + diff * diff
                weight = weight * lax.rsqrt(square)
            denom = denom + weight
            numer = [n + weight * v for n, v in zip(numer, values)]
        scale = 1.0 / (over_dates(denom) + 1.0)
        median = [(over_dates(n) + m) * scale for n, m in zip(numer, median)]
    for b in range(bands):
        gath[core, x, z, b] = median[b][0:2]
        square = median[b] * median[b]
        part[b : b + 1, :] = median[b][0:1] + median[b][1:2]
        part[bands + b : bands + b + 1, :] = square[0:1] + square[1:2]

    def pass_on(chunk, send_sem, recv_sem, to):
        pltpu.make_async_remote_copy(
            src_ref=gath.at[chunk], dst_ref=gath.at[chunk],
            send_sem=send_sem, recv_sem=recv_sem,
            device_id={"date": to}, device_id_type=MESH,
        ).start()

    for zz in (0, 1, 7, 2, 6, 3, 5, 4):

        @pl.when(zz != z)
        def _():
            pass_on((core, x, z), s_z, r_z.at[z], date_at(zz, x, core))

    def along_x(zz):
        for xx in (0, 1, 3, 2):

            @pl.when(xx != x)
            def _():
                pass_on((core, x, zz), s_x, r_x.at[zz], date_at(z, xx, core))

    distant = (z >= 3) & (z <= 5) & (x != 0) & (core == 0)

    @pl.when(distant)
    def _():
        pass_on((core, x, z), s_far, r_core.at[1], ELDEST)

    along_x(z)
    pass_on((core, x, z), s_core, r_core.at[0], date_at(z, x, 1 - core))

    sums = jnp.sum(part[...], axis=1, keepdims=True)
    lane = lax.broadcasted_iota(jnp.int32, (2 * bands, LANES), 1)
    which = lax.broadcasted_iota(jnp.int32, (2 * bands, LANES), 0)
    ymom[y] = jnp.sum(jnp.where(lane == which, sums, 0.0), axis=0, keepdims=True)
    for step in range(1, Y):
        pltpu.make_async_remote_copy(
            src_ref=ymom.at[y], dst_ref=ymom.at[y], send_sem=s_ymom, recv_sem=r_ymom,
            device_id={"pix": (y + step) % Y}, device_id_type=MESH,
        ).start()

    eldest = (me == ELDEST) & (y == 0)
    others = (me != ELDEST) | (y != 0)
    every[y * PEERS + me] = ymom[y]

    @pl.when(others)
    def _():
        pltpu.make_async_remote_copy(
            src_ref=every.at[y * PEERS + me], dst_ref=every.at[y * PEERS + me], send_sem=s_every, recv_sem=r_every,
            device_id={"date": ELDEST, "pix": 0}, device_id_type=MESH,
        ).start()
    def spread(step):
        zz = (z + step) % Z
        taken(gath.at[core, x], 1, r_z.at[zz])
        chunk = (core, x, zz)
        along_x(zz)
        pass_on(chunk, s_core, r_core.at[int(step in (3, 5, 4))], date_at(z, x, 1 - core))

    spread(1)
    spread(7)
    taken(ymom, Y - 1, r_ymom)
    dmom[me] = (ymom[0] + ymom[1]) + (ymom[2] + ymom[3])

    @pl.loop(0, PEERS)
    def _(to):
        @pl.when((to != me) & ((to != ELDEST) | (y != 0)))
        def _():
            pltpu.make_async_remote_copy(
                src_ref=dmom.at[me], dst_ref=dmom.at[me], send_sem=s_dmom, recv_sem=r_dmom,
                device_id={"date": to}, device_id_type=MESH,
            ).start()

    for step in (2, 6, 3, 5, 4):
        spread(step)
    elsewhere = (z != 0) | (x != 0) | (core != 0)
    for step in (0, 1, 7, 2, 6, 3, 5, 4):
        zz = (z + step) % Z
        taken(gath.at[core, x], X - 1, r_x.at[zz])

        def hand_over(send_sem):
            for hop in (1, 3, 2):
                pass_on((core, (x + hop) % X, zz), send_sem, r_core.at[int(step in (3, 5, 4))], date_at(z, x, 1 - core))

        if step in (3, 5, 4):

            @pl.when(elsewhere)
            def _():
                hand_over(s_late)

        else:
            hand_over(s_mid)

    @pl.when(others)
    def _():
        taken(dmom, PEERS - 1, r_dmom)
        total = dmom[0]
        for d in range(1, PEERS):
            total = total + dmom[d]
        whole[...] = total

    @pl.when(eldest)
    def _():
        taken(every, Y * PEERS - 1, r_every)

        def of_date(d):
            return (every[d] + every[PEERS + d]) + (every[2 * PEERS + d] + every[3 * PEERS + d])

        total = of_date(0)
        for d in range(1, PEERS):
            total = total + of_date(d)
        whole[...] = total

    total = whole[...]
    lane = lax.broadcasted_iota(jnp.int32, (1, LANES), 1)
    means, scales = [], []
    for b in range(bands):
        mean = jnp.sum(jnp.where(lane == b, total, 0.0), axis=1, keepdims=True) / pixels
        second = jnp.sum(jnp.where(lane == bands + b, total, 0.0), axis=1, keepdims=True) / pixels
        var = second - mean * mean
        means.append(mean)
        scales.append(1.0 / jnp.sqrt(var + EPS))

    def settle(cc, start, count):
        @pl.loop(0, count)
        def _(step):
            zz = (z + start + step) % Z
            tile = pl.ds(pl.multiple_of((zz * CORE + cc) * LANES, LANES), LANES)
            for b in range(bands):
                block = jnp.concatenate([gath[cc, k, zz, b] for k in range(PAIRS)], axis=0)
                out_ref[b, :, tile] = (block - means[b]) * scales[b]

    settle(core, 0, Z)
    for group, start, count in ((0, Z - 2, 5), (1, 3, 3)):
        part_of = gath.at[0, :, pl.ds(0, count)]
        pltpu.make_async_copy(part_of, part_of, r_core.at[group]).wait()
        settle(1 - core, start, count)

    taken(send, PEERS - 1, s_stack)
    taken(vsend, PEERS - 1, s_valid)
    @pl.when(others & (y == 0))
    def _():
        taken(dmom, PEERS - 2, s_dmom)

    @pl.when(eldest | (y != 0))
    def _():
        taken(dmom, PEERS - 1, s_dmom)

    @pl.when(others)
    def _():
        taken(every, 1, s_every)

    taken(ymom, Y - 1, s_ymom)
    taken(gath.at[0, 0], Z - 1, s_z)
    taken(gath.at[0], X - 1, s_x)
    taken(gath.at[0], 1, s_core)
    mid = gath.at[0, pl.ds(0, X - 1), pl.ds(0, Z - 3)]
    pltpu.make_async_copy(mid, mid, s_mid).wait()

    @pl.when(elsewhere)
    def _():
        late = gath.at[0, pl.ds(0, X - 1), pl.ds(0, 3)]
        pltpu.make_async_copy(late, late, s_late).wait()

    @pl.when(distant)
    def _():
        taken(gath.at[0, 0], 1, s_far)


def body(stack, cloud):
    _, bands, rows, cols = stack.shape
    pixels = float(lax.axis_size("pix") * rows * cols)
    f32, bf16 = jnp.float32, jnp.bfloat16
    dma = pltpu.SemaphoreType.DMA
    return pl.pallas_call(
        functools.partial(kernel, pixels),
        out_shape=jax.ShapeDtypeStruct((bands, rows, cols), f32),
        in_specs=[pl.BlockSpec(memory_space=pltpu.HBM)] * 2,
        out_specs=pl.BlockSpec(memory_space=pltpu.VMEM),
        scratch_shapes=[
            pltpu.VMEM((bands, rows, cols), bf16),
            pltpu.VMEM((rows, cols), jnp.int32),
            pltpu.VMEM((PEERS, bands, 2, LANES), bf16),
            pltpu.VMEM((PEERS, bands, 2, LANES), bf16),
            pltpu.VMEM((2, 1, cols), f32),
            pltpu.VMEM((2, 1, cols), f32),
            pltpu.VMEM((PEERS, 2, LANES), bf16),
            pltpu.VMEM((PEERS, 2, LANES), bf16),
            pltpu.VMEM((bands, 2 * PEERS, LANES), f32),
            pltpu.VMEM((2 * PEERS, LANES), f32),
            pltpu.VMEM((CORE, X, Z, bands, 2, LANES), f32),
            pltpu.VMEM((2 * bands, LANES), f32),
            pltpu.VMEM((Y, 1, LANES), f32),
            pltpu.VMEM((PEERS, 1, LANES), f32),
            pltpu.VMEM((Y * PEERS, 1, LANES), f32),
            pltpu.VMEM((1, LANES), f32),
            dma, dma((Z,)), dma((2,)), dma((2,)), dma, dma,
            dma, dma, dma, dma((Z,)), dma((Z,)), dma((2,)), dma, dma, dma, dma,
            dma((2,)), pltpu.SemaphoreType.REGULAR((3,)), dma, dma, dma, dma, dma,
        ],
        compiler_params=pltpu.CompilerParams(collective_id=0, has_side_effects=True, vmem_limit_bytes=8 << 20),
    )(pltpu.with_memory_space_constraint(stack[0], pltpu.HBM), pltpu.with_memory_space_constraint(cloud[0], pltpu.HBM))


def solution(mesh):
    placed = (P("date", None, "pix", None), P("date", "pix", None))
    return jax.shard_map(
        body, mesh=mesh, in_specs=placed, out_specs=P(None, "pix", None), check_vma=False
    )
```

```python
import functools

import jax
import jax.numpy as jnp
from jax import lax
from jax.experimental import pallas as pl
from jax.experimental.pallas import tpu as pltpu
from jax.sharding import PartitionSpec as P

ITERS = 2
DELTA_SQ = 0.01
EPS = 1e-05
MESH = pl.DeviceIdType.MESH
Z, X, CORE, Y = 8, 4, 2, 4
LINE = X * CORE
PEERS = Z * LINE
PAIRS = 4
ELDEST = 1
LANES = 128


def kernel(
    pixels, stack_hbm, cloud_hbm, out_ref,
    stack_ref, cloud_ref, send, recv, hsend, hrecv, vsend, vrecv, work, seen, gath, part, ymom, dmom, every, whole,
    s_stack, r_stack, s_halo, r_halo, s_valid, r_valid,
    s_z, s_x, s_core, r_z, r_x, r_core, s_ymom, r_ymom, s_dmom, r_dmom,
    s_in, far, s_every, r_every, s_mid, s_late, s_far,
):
    bands = stack_ref.shape[0]
    rows, cols = cloud_ref.shape
    me = lax.axis_index("date")
    y = lax.axis_index("pix")
    z = me // (X * CORE)
    x = (me // CORE) % X
    core = me % CORE

    def date_at(zz, xx, cc):
        return (zz * X + xx) * CORE + cc

    def peer(step):
        return (me + step) % PEERS

    def in_line(zz, step):
        return zz * LINE + (me % LINE + step) % LINE

    def give(zz, first):
        @pl.loop(first, LINE)
        def _(step):
            to = in_line(zz, step)
            pltpu.make_async_remote_copy(
                src_ref=send.at[to], dst_ref=recv.at[me],
                send_sem=s_stack, recv_sem=r_stack.at[z],
                device_id={"date": to}, device_id_type=MESH,
            ).start()

    fetches = [
        pltpu.make_async_copy(cloud_hbm, cloud_ref, s_in.at[0]),
        pltpu.make_async_copy(stack_hbm, stack_ref, s_in.at[1]),
    ]

    barrier = pltpu.get_barrier_semaphore()
    for copy in fetches:
        copy.start()

    def greet(zz, first):
        @pl.loop(first, LINE)
        def _(step):
            pl.semaphore_signal(
                barrier, inc=1, device_id={"date": in_line(zz, step)}, device_id_type=MESH
            )

    for dz in (2, 6, 1, 7):
        greet((z + dz) % Z, 0)
    greet(z, 1)

    for step in range(1, Y):
        pl.semaphore_signal(barrier, inc=1, device_id={"pix": (y + step) % Y}, device_id_type=MESH)

    for copy in fetches:
        copy.wait()

    @pl.loop(0, Z)
    def _(zz):
        for cc in range(CORE):
            tile = pl.ds(pl.multiple_of((zz * CORE + cc) * LANES, LANES), LANES)
            for k in range(PAIRS):
                send[date_at(zz, k, cc)] = stack_ref[:, 2 * k : 2 * k + 2, tile]

    recv[me] = send[me]
    cloudy = (1 - cloud_ref[...]).astype(jnp.float32)
    hsend[0] = cloudy[0:1]
    hsend[1] = cloudy[rows - 1 : rows]

    pl.semaphore_wait(barrier, 5 * LINE - 1 + Y - 1)
    for slot, dz in enumerate((Z - 1, 1, Z - 2)):
        to = date_at((z + dz) % Z, x, core)
        pl.semaphore_signal(far.at[slot], inc=1, device_id={"date": to}, device_id_type=MESH)

    halos = []
    for side, to in ((0, (y + Y - 1) % Y), (1, (y + 1) % Y)):
        halos.append(
            pltpu.make_async_remote_copy(
                src_ref=hsend.at[side], dst_ref=hrecv.at[side],
                send_sem=s_halo, recv_sem=r_halo,
                device_id={"pix": to}, device_id_type=MESH,
            )
        )
    for copy in halos:
        copy.start()

    for dz in (2, 6):
        give((z + dz) % Z, 0)
    for slot, dz in enumerate((3, 5, 4)):
        pl.semaphore_wait(far.at[slot], 1)
        give((z + dz) % Z, 0)

    pltpu.make_async_copy(hsend, hsend, s_halo).wait()
    pltpu.make_async_copy(hrecv, hrecv, r_halo).wait()
    above = jnp.where(y > 0, hrecv[1], 0.0)
    below = jnp.where(y < Y - 1, hrecv[0], 0.0)
    row = lax.broadcasted_iota(jnp.int32, (rows, cols), 0)
    col = lax.broadcasted_iota(jnp.int32, (rows, cols), 1)
    near = jnp.maximum(cloudy, jnp.where(row == 0, above, pltpu.roll(cloudy, 1, 0)))
    near = jnp.maximum(near, jnp.where(row == rows - 1, below, pltpu.roll(cloudy, rows - 1, 0)))
    near = jnp.maximum(near, jnp.where(col == 0, 0.0, pltpu.roll(cloudy, 1, 1)))
    near = jnp.maximum(near, jnp.where(col == cols - 1, 0.0, pltpu.roll(cloudy, cols - 1, 1)))
    valid = 1.0 - near
    for c in range(Z * CORE):
        for k in range(PAIRS):
            block = valid[2 * k : 2 * k + 2, c * LANES : (c + 1) * LANES]
            vsend[date_at(c // CORE, k, c % CORE)] = block.astype(jnp.bfloat16)
    vrecv[me] = vsend[me]

    @pl.loop(1, PEERS)
    def _(step):
        to = peer(step)
        pltpu.make_async_remote_copy(
            src_ref=vsend.at[to], dst_ref=vrecv.at[me], send_sem=s_valid, recv_sem=r_valid,
            device_id={"date": to}, device_id_type=MESH,
        ).start()

    for dz in (1, 7):
        give((z + dz) % Z, 0)
    give(z, 1)

    def taken(ref, count, sem):
        some = ref.at[pl.ds(0, count)]
        pltpu.make_async_copy(some, some, sem).wait()

    def rows_of(zz):
        return pl.ds(pl.multiple_of(2 * LINE * zz, 2 * LINE), 2 * LINE)

    def unpack(zz):
        for step in range(LINE):
            block = recv[zz * LINE + step].astype(jnp.float32)
            for b in range(bands):
                work.at[b, rows_of(zz)][2 * step : 2 * step + 2, :] = block[b]

    @pl.loop(2, Z - 1)
    def _(step):
        zz = (z + step) % Z
        taken(recv, LINE, r_stack.at[zz])
        unpack(zz)

    for step in (1, Z - 1):
        zz = (z + step) % Z
        taken(recv, LINE, r_stack.at[zz])
        unpack(zz)

    taken(recv, LINE - 1, r_stack.at[z])
    unpack(z)

    taken(vrecv, PEERS - 1, r_valid)

    @pl.loop(0, Z)
    def _(zz):
        for step in range(LINE):
            block = vrecv[zz * LINE + step].astype(jnp.float32)
            seen.at[rows_of(zz)][2 * step : 2 * step + 2, :] = block

    def over_dates(sums):
        sums = sums + pltpu.roll(sums, 2, 0)
        return sums + pltpu.roll(sums, 4, 0)

    median = [jnp.zeros((8, LANES), jnp.float32)] * bands
    for step in range(ITERS + 1):
        numer = [jnp.zeros((8, LANES), jnp.float32)] * bands
        denom = jnp.zeros((8, LANES), jnp.float32)
        for j in range(0, 2 * PEERS, 8):
            values = [work[b, j : j + 8, :] for b in range(bands)]
            weight = seen[j : j + 8, :]
            if step > 0:
                square = DELTA_SQ
                for b in range(bands):
                    diff = values[b] - median[b]
                    square = square + diff * diff
                weight = weight * lax.rsqrt(square)
            denom = denom + weight
            numer = [n + weight * v for n, v in zip(numer, values)]
        scale = 1.0 / (over_dates(denom) + 1.0)
        median = [(over_dates(n) + m) * scale for n, m in zip(numer, median)]
    for b in range(bands):
        gath[core, x, z, b] = median[b][0:2]
        square = median[b] * median[b]
        part[b : b + 1, :] = median[b][0:1] + median[b][1:2]
        part[bands + b : bands + b + 1, :] = square[0:1] + square[1:2]

    def pass_on(chunk, send_sem, recv_sem, to):
        pltpu.make_async_remote_copy(
            src_ref=gath.at[chunk], dst_ref=gath.at[chunk],
            send_sem=send_sem, recv_sem=recv_sem,
            device_id={"date": to}, device_id_type=MESH,
        ).start()

    for zz in (0, 1, 7, 2, 6, 3, 5, 4):

        @pl.when(zz != z)
        def _():
            pass_on((core, x, z), s_z, r_z.at[z], date_at(zz, x, core))

    def along_x(zz):
        for xx in (0, 1, 3, 2):

            @pl.when(xx != x)
            def _():
                pass_on((core, x, zz), s_x, r_x.at[zz], date_at(z, xx, core))

    distant = (z >= 3) & (z <= 5) & (x != 0) & (core == 0)

    @pl.when(distant)
    def _():
        pass_on((core, x, z), s_far, r_core, ELDEST)

    along_x(z)
    pass_on((core, x, z), s_core, r_core, date_at(z, x, 1 - core))

    sums = jnp.sum(part[...], axis=1, keepdims=True)
    lane = lax.broadcasted_iota(jnp.int32, (2 * bands, LANES), 1)
    which = lax.broadcasted_iota(jnp.int32, (2 * bands, LANES), 0)
    ymom[y] = jnp.sum(jnp.where(lane == which, sums, 0.0), axis=0, keepdims=True)
    for step in range(1, Y):
        pltpu.make_async_remote_copy(
            src_ref=ymom.at[y], dst_ref=ymom.at[y], send_sem=s_ymom, recv_sem=r_ymom,
            device_id={"pix": (y + step) % Y}, device_id_type=MESH,
        ).start()

    eldest = (me == ELDEST) & (y == 0)
    others = (me != ELDEST) | (y != 0)
    every[y * PEERS + me] = ymom[y]

    @pl.when(others)
    def _():
        pltpu.make_async_remote_copy(
            src_ref=every.at[y * PEERS + me], dst_ref=every.at[y * PEERS + me], send_sem=s_every, recv_sem=r_every,
            device_id={"date": ELDEST, "pix": 0}, device_id_type=MESH,
        ).start()
    def spread(step):
        zz = (z + step) % Z
        taken(gath.at[core, x], 1, r_z.at[zz])
        chunk = (core, x, zz)
        along_x(zz)
        pass_on(chunk, s_core, r_core, date_at(z, x, 1 - core))

    spread(1)
    spread(7)
    taken(ymom, Y - 1, r_ymom)
    dmom[me] = (ymom[0] + ymom[1]) + (ymom[2] + ymom[3])

    @pl.loop(0, PEERS)
    def _(to):
        @pl.when((to != me) & ((to != ELDEST) | (y != 0)))
        def _():
            pltpu.make_async_remote_copy(
                src_ref=dmom.at[me], dst_ref=dmom.at[me], send_sem=s_dmom, recv_sem=r_dmom,
                device_id={"date": to}, device_id_type=MESH,
            ).start()

    for step in (2, 6, 3, 5, 4):
        spread(step)
    elsewhere = (z != 0) | (x != 0) | (core != 0)
    for step in (0, 1, 7, 2, 6, 3, 5, 4):
        zz = (z + step) % Z
        taken(gath.at[core, x], X - 1, r_x.at[zz])

        def hand_over(send_sem):
            for hop in (1, 3, 2):
                pass_on((core, (x + hop) % X, zz), send_sem, r_core, date_at(z, x, 1 - core))

        if step in (3, 5, 4):

            @pl.when(elsewhere)
            def _():
                hand_over(s_late)

        else:
            hand_over(s_mid)

    @pl.when(others)
    def _():
        taken(dmom, PEERS - 1, r_dmom)
        total = dmom[0]
        for d in range(1, PEERS):
            total = total + dmom[d]
        whole[...] = total

    @pl.when(eldest)
    def _():
        taken(every, Y * PEERS - 1, r_every)

        def of_date(d):
            return (every[d] + every[PEERS + d]) + (every[2 * PEERS + d] + every[3 * PEERS + d])

        total = of_date(0)
        for d in range(1, PEERS):
            total = total + of_date(d)
        whole[...] = total

    total = whole[...]
    lane = lax.broadcasted_iota(jnp.int32, (1, LANES), 1)
    means, scales = [], []
    for b in range(bands):
        mean = jnp.sum(jnp.where(lane == b, total, 0.0), axis=1, keepdims=True) / pixels
        second = jnp.sum(jnp.where(lane == bands + b, total, 0.0), axis=1, keepdims=True) / pixels
        var = second - mean * mean
        means.append(mean)
        scales.append(1.0 / jnp.sqrt(var + EPS))

    def settle(cc):
        @pl.loop(0, Z)
        def _(zz):
            tile = pl.ds(pl.multiple_of((zz * CORE + cc) * LANES, LANES), LANES)
            for b in range(bands):
                block = jnp.concatenate([gath[cc, k, zz, b] for k in range(PAIRS)], axis=0)
                out_ref[b, :, tile] = (block - means[b]) * scales[b]

    settle(core)
    pltpu.make_async_copy(gath.at[0], gath.at[0], r_core).wait()
    settle(1 - core)

    taken(send, PEERS - 1, s_stack)
    taken(vsend, PEERS - 1, s_valid)
    @pl.when(others & (y == 0))
    def _():
        taken(dmom, PEERS - 2, s_dmom)

    @pl.when(eldest | (y != 0))
    def _():
        taken(dmom, PEERS - 1, s_dmom)

    @pl.when(others)
    def _():
        taken(every, 1, s_every)

    taken(ymom, Y - 1, s_ymom)
    taken(gath.at[0, 0], Z - 1, s_z)
    taken(gath.at[0], X - 1, s_x)
    taken(gath.at[0], 1, s_core)
    mid = gath.at[0, pl.ds(0, X - 1), pl.ds(0, Z - 3)]
    pltpu.make_async_copy(mid, mid, s_mid).wait()

    @pl.when(elsewhere)
    def _():
        late = gath.at[0, pl.ds(0, X - 1), pl.ds(0, 3)]
        pltpu.make_async_copy(late, late, s_late).wait()

    @pl.when(distant)
    def _():
        taken(gath.at[0, 0], 1, s_far)


def body(stack, cloud):
    _, bands, rows, cols = stack.shape
    pixels = float(lax.axis_size("pix") * rows * cols)
    f32, bf16 = jnp.float32, jnp.bfloat16
    dma = pltpu.SemaphoreType.DMA
    return pl.pallas_call(
        functools.partial(kernel, pixels),
        out_shape=jax.ShapeDtypeStruct((bands, rows, cols), f32),
        in_specs=[pl.BlockSpec(memory_space=pltpu.HBM)] * 2,
        out_specs=pl.BlockSpec(memory_space=pltpu.VMEM),
        scratch_shapes=[
            pltpu.VMEM((bands, rows, cols), bf16),
            pltpu.VMEM((rows, cols), jnp.int32),
            pltpu.VMEM((PEERS, bands, 2, LANES), bf16),
            pltpu.VMEM((PEERS, bands, 2, LANES), bf16),
            pltpu.VMEM((2, 1, cols), f32),
            pltpu.VMEM((2, 1, cols), f32),
            pltpu.VMEM((PEERS, 2, LANES), bf16),
            pltpu.VMEM((PEERS, 2, LANES), bf16),
            pltpu.VMEM((bands, 2 * PEERS, LANES), f32),
            pltpu.VMEM((2 * PEERS, LANES), f32),
            pltpu.VMEM((CORE, X, Z, bands, 2, LANES), f32),
            pltpu.VMEM((2 * bands, LANES), f32),
            pltpu.VMEM((Y, 1, LANES), f32),
            pltpu.VMEM((PEERS, 1, LANES), f32),
            pltpu.VMEM((Y * PEERS, 1, LANES), f32),
            pltpu.VMEM((1, LANES), f32),
            dma, dma((Z,)), dma, dma, dma, dma,
            dma, dma, dma, dma((Z,)), dma((Z,)), dma, dma, dma, dma, dma,
            dma((2,)), pltpu.SemaphoreType.REGULAR((3,)), dma, dma, dma, dma, dma,
        ],
        compiler_params=pltpu.CompilerParams(collective_id=0, has_side_effects=True, vmem_limit_bytes=8 << 20),
    )(pltpu.with_memory_space_constraint(stack[0], pltpu.HBM), pltpu.with_memory_space_constraint(cloud[0], pltpu.HBM))


def solution(mesh):
    placed = (P("date", None, "pix", None), P("date", "pix", None))
    return jax.shard_map(
        body, mesh=mesh, in_specs=placed, out_specs=P(None, "pix", None), check_vma=False
    )
```
